32 devices in a mesh: group: 16 (over z, x, core), rep: 2 (over y).
Axes of the slice: x: 2, y: 2, z: 4, core: 2. Of those that a mesh axis runs over, the one named last changes fastest.
Arguments:
- queries: bfloat16 [32, 256, 3072], P(('group', 'rep')), may hold values from -46 to 46
- keys: bfloat16 [32, 256, 3072], P(('group', 'rep')), may hold values from -46 to 46
- values: bfloat16 [32, 256, 3072], P(('group', 'rep')), may hold values from -6 to 6
- grad_output: bfloat16 [32, 256, 3072], P(('group', 'rep')), may hold values from -6 to 6
- weight_codes: bfloat16 [3072, 3072], P('group'), may hold values from -4 to 4
- weight_scales: float32 [3072, 12], P('group'), may hold values from 0.006 to 0.06
Outputs:
- grad_queries: bfloat16 [32, 256, 3072], P(('group', 'rep'))
- grad_keys: bfloat16 [32, 256, 3072], P(('group', 'rep'))
- grad_values: bfloat16 [32, 256, 3072], P(('group', 'rep'))
- grad_weight: float32 [3072, 3072], P(('group', 'rep'))
The draws below stay inside these ranges and needn't reach their ends.
All inputs are finite; a program needn't handle non-finite values.
Results may differ from the reference program's by a relative error of at most 0.029.
Values may be sent and summed in bfloat16 or wider, within the bound.
A program may use at most 128 MiB of HBM per device.

```python
import math
import jax
import jax.numpy as jnp
from jax import lax

H = 24
HD = 128
E = 3072
BLOCK = 256
SEQ = 256
IMG_DEV = 1
ROWS = 3072
IMAGES = 32
N_GROUP = 16
N_REP = 2


def make_pairs(key):
    base = jax.random.fold_in(key, 7)
    key_query, key_keys = jax.random.split(base, 2)
    shape = (IMAGES, SEQ, H, HD)
    query = jnp.clip(jax.random.normal(key_query, shape, jnp.float32), -4.0, 4.0)
    keyset = jnp.clip(jax.random.normal(key_keys, shape, jnp.float32), -4.0, 4.0)
    query = query.reshape(IMAGES, SEQ, H * HD).astype(jnp.bfloat16)
    keyset = keyset.reshape(IMAGES, SEQ, H * HD).astype(jnp.bfloat16)
    return (query, keyset)


def draw_queries(key, part):
    return make_pairs(key)[0]


def draw_keys(key, part):
    return make_pairs(key)[1]


def with_spikes(result, stream_key, source, target, shards_of, factor):
    owner, partner = [(jnp.arange(result.shape[dim]) // (result.shape[dim] // shards_of)).reshape([-1 if axis == dim else 1 for axis in range(result.ndim)]) for dim in (source, target)]
    chosen = jax.random.permutation(stream_key, shards_of)[partner]
    strong = (owner == chosen) | (owner == (partner + shards_of // 2) % shards_of)
    return jnp.where(strong, factor * result, result)


def block_levels(key, extent, shards, low, top_value):
    loudness, own = 1.0, jax.random.fold_in(key, 6)
    for position, shards_of in shards:
        steps = jnp.exp(jax.random.uniform(jax.random.fold_in(own, position), (shards_of,), jnp.float32, low / len(shards), top_value / len(shards)))
        loudness = loudness * jnp.repeat(steps, extent[position] // shards_of).reshape([-1 if axis == position else 1 for axis in range(len(extent))])
    return loudness


def bell_draw(key, dims, deviation, most, shards=(), kind=jnp.bfloat16):
    loudness = block_levels(key, dims, shards, -0.22, 0.18) if shards else 1.0
    entries = jax.random.normal(key, dims, jnp.float32) * deviation * loudness
    return jnp.minimum(jnp.maximum(entries, -most), most).astype(kind)


def bell_draw_with(key, extent, scale, reach, cuts, heavy, dtype=jnp.bfloat16):
    values = scale * jax.random.normal(key, extent, jnp.float32)
    if cuts:
        values = values * block_levels(key, extent, cuts, -0.22, 0.18)
    return jnp.clip(with_spikes(values, jax.random.fold_in(key, 3), *heavy), -reach, reach).astype(dtype)


def setup_inputs(seed: int = 0) -> dict:
    key_of = jax.random.split(jax.random.key(seed), 7)
    return {
        "queries": draw_queries(jax.random.fold_in(key_of[6], 71), 0),
        "keys": draw_keys(jax.random.fold_in(key_of[6], 71), 0),
        "values": bell_draw_with(key_of[2], (IMAGES, SEQ, ROWS), 1.0, 6.0, ((0, 32),), (0, 2, 32, 2.75)),
        "grad_output": bell_draw(key_of[3], (IMAGES, SEQ, E), 1.0, 6.0, ((0, 32),)),
        "weight_codes": bell_draw(key_of[4], (ROWS, E), 1.0, 4.0, ((0, 16),)),
        "weight_scales": jnp.clip(jnp.exp(math.log(0.06) - 2.3025851 * jax.random.uniform(key_of[5], (ROWS, E // BLOCK), jnp.float32) ** block_levels(key_of[5], (ROWS, E // BLOCK), ((0, 16),), -0.2, 0.2)), 0.006, 0.06),
    }


def forward_image(arrays_in):
    query, keyset, valueset = arrays_in
    seq_len = query.shape[0]
    query_heads = query.astype(jnp.float32).reshape(seq_len, H, HD)
    key_heads = keyset.astype(jnp.float32).reshape(seq_len, H, HD)
    value_heads = valueset.astype(jnp.float32).reshape(seq_len, H, HD)
    scores = jnp.einsum("qhd,khd->hqk", query_heads, key_heads) * HD ** -0.5
    highest = jnp.max(scores, axis=2, keepdims=True)
    exponent = jnp.exp(scores - highest)
    probability = exponent / jnp.sum(exponent, axis=2, keepdims=True)
    weight_half = probability.astype(jnp.bfloat16)
    context = jnp.einsum("hqk,khd->qhd", weight_half.astype(jnp.float32), value_heads).astype(jnp.bfloat16)
    return probability, weight_half, context.reshape(seq_len, H * HD)


def context_only(arrays_in):
    return forward_image(arrays_in)[2]


def backward_image(arrays_in):
    query, keyset, valueset, grad_context = arrays_in
    seq_len = query.shape[0]
    probability, weight_half, context = forward_image((query, keyset, valueset))
    query_heads = query.astype(jnp.float32).reshape(seq_len, H, HD)
    key_heads = keyset.astype(jnp.float32).reshape(seq_len, H, HD)
    value_heads = valueset.astype(jnp.float32).reshape(seq_len, H, HD)
    grad_heads = grad_context.astype(jnp.float32).reshape(seq_len, H, HD)
    grad_value = jnp.einsum("hqk,qhd->khd", weight_half.astype(jnp.float32), grad_heads).astype(jnp.bfloat16)
    dprobs = jnp.einsum("qhd,khd->hqk", grad_heads, value_heads)
    row_delta = jnp.sum(probability * dprobs, axis=2, keepdims=True)
    dscores = (probability * (dprobs - row_delta) * HD ** -0.5).astype(jnp.bfloat16).astype(jnp.float32)
    grad_query = jnp.einsum("hqk,khd->qhd", dscores, key_heads).astype(jnp.bfloat16)
    grad_key = jnp.einsum("hqk,qhd->khd", dscores, query_heads).astype(jnp.bfloat16)
    return (grad_query.reshape(seq_len, H * HD), grad_key.reshape(seq_len, H * HD), grad_value.reshape(seq_len, H * HD))


def reference(queries, keys, values, grad_output, weight_codes, weight_scales):
    scaled = weight_codes.astype(jnp.float32).reshape(ROWS, E // BLOCK, BLOCK) * weight_scales[:, :, None]
    weight = scaled.reshape(ROWS, E).astype(jnp.bfloat16)
    contexts = lax.map(context_only, (queries, keys, values))
    grad_flat = jnp.dot(grad_output.reshape(IMAGES * SEQ, E), weight.T, preferred_element_type=jnp.float32)
    grad_context = grad_flat.astype(jnp.bfloat16).reshape(IMAGES, SEQ, ROWS)
    block_total = N_GROUP * N_REP
    context_blocks = contexts.reshape(block_total, IMG_DEV * SEQ, ROWS)
    output_blocks = grad_output.reshape(block_total, IMG_DEV * SEQ, E)

    def add_block(running, pair):
        term = jnp.dot(pair[0].T, pair[1], preferred_element_type=jnp.float32).astype(jnp.bfloat16)
        return running + lax.optimization_barrier(term).astype(jnp.float32), None

    grad_weight, unused = lax.scan(add_block, jnp.zeros((ROWS, E), jnp.float32), (context_blocks, output_blocks))
    grad_queries, grad_keys, grad_values = lax.map(backward_image, (queries, keys, values, grad_context))
    return grad_queries, grad_keys, grad_values, grad_weight
```

```python
import functools
import itertools
import math

import jax
import jax.numpy as jnp
from jax import lax
from jax.experimental import pallas as pl
from jax.experimental.pallas import tpu as pltpu
from jax.sharding import Mesh, PartitionSpec as P

HD = 128
SCALE = HD ** (-0.5)
CORES = 2
PLANE = ("x", "core", "rep")


def dot(a, b, dims):
    return lax.dot_general(a, b, (dims, ((), ())), preferred_element_type=jnp.float32)


def probs_t(query, keyset):
    scores = dot(keyset, query, ((1,), (1,)))
    highest = jnp.max(scores, axis=0, keepdims=True)
    exponent = jnp.exp2((scores - highest) * (SCALE * math.log2(math.e)))
    return exponent * (1.0 / jnp.sum(exponent, axis=0, keepdims=True))


def forward_kernel(heads, q_ref, k_ref, v_ref, ctx_ref):
    for head in range(heads):
        cols = slice(head * HD, (head + 1) * HD)
        prob = probs_t(q_ref[:, cols], k_ref[:, cols]).astype(jnp.bfloat16)
        ctx_ref[cols, :] = dot(v_ref[:, cols], prob, ((0,), (0,))).astype(jnp.bfloat16)


def backward_kernel(heads, q_ref, k_ref, v_ref, g_ref, dq_ref, dk_ref, dv_ref):
    for head in range(heads):
        cols = slice(head * HD, (head + 1) * HD)
        query, keyset, grad = q_ref[:, cols], k_ref[:, cols], g_ref[cols, :]
        prob = probs_t(query, keyset)
        dv_ref[:, cols] = dot(prob.astype(jnp.bfloat16), grad, ((1,), (1,))).astype(jnp.bfloat16)
        dprob = dot(v_ref[:, cols], grad, ((1,), (0,)))
        delta = jnp.sum(prob * dprob, axis=0, keepdims=True)
        dscore = (prob * (dprob - delta) * SCALE).astype(jnp.bfloat16)
        dk_ref[:, cols] = dot(dscore, query, ((1,), (0,))).astype(jnp.bfloat16)
        dq_ref[:, cols] = dot(dscore, keyset, ((0,), (0,))).astype(jnp.bfloat16)


def heads_per_step(head_count):
    return next(n for n in (4, 3, 2, 1) if head_count % n == 0)


def forward(query, keyset, valueset):
    seq, rows = query.shape
    heads = heads_per_step(rows // HD)
    wide = pl.BlockSpec((seq, heads * HD), lambda i: (0, i))
    return pl.pallas_call(
        functools.partial(forward_kernel, heads),
        grid=(rows // (heads * HD),),
        in_specs=[wide] * 3,
        out_specs=pl.BlockSpec((heads * HD, seq), lambda i: (i, 0)),
        out_shape=jax.ShapeDtypeStruct((rows, seq), jnp.bfloat16),
        cost_estimate=pl.CostEstimate(
            flops=4 * seq * seq * rows,
            bytes_accessed=8 * seq * rows,
            transcendentals=seq * seq * rows // HD,
        ),
        name="forward",
    )(query, keyset, valueset)


def backward(query, keyset, valueset, grad_t):
    seq, rows = query.shape
    heads = heads_per_step(rows // HD)
    wide = pl.BlockSpec((seq, heads * HD), lambda i: (0, i))
    return pl.pallas_call(
        functools.partial(backward_kernel, heads),
        grid=(rows // (heads * HD),),
        in_specs=[wide] * 3 + [pl.BlockSpec((heads * HD, seq), lambda i: (i, 0))],
        out_specs=[wide] * 3,
        out_shape=[jax.ShapeDtypeStruct((seq, rows), jnp.bfloat16)] * 3,
        cost_estimate=pl.CostEstimate(
            flops=10 * seq * seq * rows,
            bytes_accessed=14 * seq * rows,
            transcendentals=seq * seq * rows // HD,
        ),
        name="backward",
    )(query, keyset, valueset, grad_t)


def term_kernel(count, *refs):
    total = None
    for i in range(count):
        part = dot(refs[i][...], refs[count + i][...], ((1,), (0,)))
        total = part if total is None else total + part
    refs[-1][...] = total.astype(jnp.bfloat16)


def weight_terms(contexts, outputs):
    count = len(contexts)
    rows, seq = contexts[0].shape
    features = outputs[0].shape[1]
    tile = math.gcd(features, 512)
    return pl.pallas_call(
        functools.partial(term_kernel, count),
        grid=(features // tile,),
        in_specs=[pl.BlockSpec((rows, seq), lambda i: (0, 0))] * count
        + [pl.BlockSpec((seq, tile), lambda i: (0, i))] * count,
        out_specs=pl.BlockSpec((rows, tile), lambda i: (0, i)),
        out_shape=jax.ShapeDtypeStruct((rows, features), jnp.bfloat16),
        cost_estimate=pl.CostEstimate(
            flops=2 * rows * seq * features * count,
            bytes_accessed=2 * (count * seq * (rows + features) + rows * features),
            transcendentals=0,
        ),
        name="terms",
    )(*contexts, *outputs)


def restore(codes, scales):
    rows, blocks = scales.shape
    spread = codes.astype(jnp.float32).reshape(rows, blocks, -1) * scales[:, :, None]
    return spread.reshape(rows, -1).astype(jnp.bfloat16)


MESH_ID = pl.DeviceIdType.MESH
AXES = ("z", "x", "core", "rep")
CHUNKS = 6


def fused_kernel(
    depth,
    chunks,
    pieces,
    q_hbm,
    k_hbm,
    v_hbm,
    g_hbm,
    codes_hbm,
    scales_ref,
    dq_hbm,
    dk_hbm,
    dv_hbm,
    dw_hbm,
    ins,
    codes,
    near,
    weight,
    context,
    outgoing,
    total,
    grads_out,
    grads,
    part_out,
    part_in,
    sum_out,
    sum_in,
    own_sum,
    part,
    probs,
    results,
    in_sem,
    codes_sem,
    own_sem,
    direct_send,
    direct_recv,
    relay_send,
    relay_recv,
    ctx_send,
    ctx_recv,
    ctx_own,
    line_send,
    line_recv,
    sib_send,
    sib_recv,
    part_send,
    part_recv,
    sum_send,
    sum_recv,
    grad_send,
    grad_recv,
    grad_own,
    out_sem,
    dw_sem,
):
    z, x, c, y = (lax.axis_index(axis) for axis in AXES)
    groups, seq, width = ins.shape[1:]
    heads = width // HD
    slab = codes.shape[0]
    span = near.shape[-1]
    half = seq // 2
    across, along, corner = (z, 1 - x, c, y), (z, x, c, 1 - y), (z, 1 - x, c, 1 - y)
    sibling = (z, x, 1 - c, y)
    plane = (across, along, corner)
    owners = ((1 - x, y), (x, 1 - y), (1 - x, 1 - y))
    column = [(lax.rem(z + d, depth), x, c, y) for d in range(1, depth)]

    barrier = pltpu.get_barrier_semaphore()
    partners = [*plane, sibling, *column]
    for partner in partners:
        pl.semaphore_signal(barrier, inc=1, device_id=partner, device_id_type=MESH_ID)

    def remote(source, target, send, recv, device):
        return pltpu.make_async_remote_copy(
            src_ref=source,
            dst_ref=target,
            send_sem=send,
            recv_sem=recv,
            device_id=device,
            device_id_type=MESH_ID,
        )

    def own_rows():
        return pl.ds(pl.multiple_of(y * slab, slab), slab)

    def load(i, group):
        source = (q_hbm, k_hbm, v_hbm)[i]
        columns = pl.ds(pl.multiple_of(group * width, width), width)
        return pltpu.make_async_copy(
            source.at[:, columns], ins.at[i, group], in_sem.at[i, group]
        )

    def own_outputs(k):
        columns = pl.ds(pl.multiple_of(k * span, span), span)
        return pltpu.make_async_copy(g_hbm.at[:, columns], near.at[k, 0], own_sem.at[k])

    def direct(k, way):
        columns = pl.ds(pl.multiple_of(k * span, span), span)
        return remote(
            g_hbm.at[:, columns],
            near.at[k, 1 + way],
            direct_send.at[way, k],
            direct_recv.at[way, k],
            plane[way],
        )

    def relay(k, way):
        rows = pl.ds(way * half, half)
        return remote(
            near.at[k, 1 + way, rows],
            near.at[k, 3, rows],
            relay_send.at[way, k],
            relay_recv.at[way, k],
            plane[1 - way],
        )

    def send_context(i, level):
        a, b = owners[i]
        return remote(
            outgoing.at[a, b, level],
            context.at[level, :, :, pl.ds((1 + i) * seq, seq)],
            ctx_send.at[i, level],
            ctx_recv.at[i, level],
            plane[i],
        )

    def keep_context(level):
        return pltpu.make_async_copy(
            outgoing.at[x, y, level],
            context.at[level, :, :, pl.ds(0, seq)],
            ctx_own.at[level],
        )

    def line(up, step):
        block = z - step if up else z + step
        at = weight.at[:, 2 * block + c]
        way = 0 if up else 1
        target = (z + 1 if up else z - 1, x, c, y)
        return remote(at, at, line_send.at[way, step], line_recv.at[way, step], target)

    def line_in(up, step):
        block = z - step if up else z + step
        at = weight.at[:, 2 * block + c]
        way = 0 if up else 1
        target = (z + 1 if up else z - 1, x, c, y)
        return remote(
            at, at, line_send.at[way, step - 1], line_recv.at[way, step - 1], target
        )

    def share(block):
        at = weight.at[:, 2 * block + c]
        return remote(at, at, sib_send.at[block], sib_recv.at[block], sibling)

    def share_in(block):
        at = weight.at[:, 2 * block + 1 - c]
        return remote(at, at, sib_send.at[block], sib_recv.at[block], sibling)

    def send_line(step):
        if step < depth - 1:

            @pl.when((z - step >= 0) & (z + 1 < depth))
            def _():
                line(True, step).start()

            @pl.when((z + step < depth) & (z - 1 >= 0))
            def _():
                line(False, step).start()

    def receive_line(step):
        @pl.when(z - step >= 0)
        def _():
            line_in(True, step).wait_recv()

        @pl.when(z + step < depth)
        def _():
            line_in(False, step).wait_recv()

        send_line(step)

        @pl.when(z - step >= 0)
        def _():
            share(z - step).start()

        @pl.when(z + step < depth)
        def _():
            share(z + step).start()

    def send_part(k):
        return remote(
            part_out.at[k], part_in.at[k], part_send.at[k], part_recv.at[k], sibling
        )

    def send_sum(k, d):
        return remote(
            sum_out.at[k, column[d][0]],
            sum_in.at[k, d],
            sum_send.at[k, d],
            sum_recv.at[k, d],
            column[d],
        )

    def send_grad(i, level):
        return remote(
            grads_out.at[1 + i, level],
            grads.at[x, y, level],
            grad_send.at[i, level],
            grad_recv.at[i, level],
            plane[i],
        )

    def grad_in(i, level):
        a, b = owners[i]
        return remote(
            grads_out.at[1 + i, level],
            grads.at[a, b, level],
            grad_send.at[i, level],
            grad_recv.at[i, level],
            plane[i],
        )

    def keep_grad(level):
        return pltpu.make_async_copy(
            grads_out.at[0, level], grads.at[x, y, level], grad_own.at[level]
        )

    def store(i, group):
        target = (dq_hbm, dk_hbm, dv_hbm)[i]
        columns = pl.ds(pl.multiple_of(group * width, width), width)
        return pltpu.make_async_copy(
            results.at[i, group], target.at[:, columns], out_sem.at[i, group]
        )

    take_codes = pltpu.make_async_copy(codes_hbm.at[own_rows()], codes, codes_sem)
    take_codes.start()
    for group in range(groups):
        for i in range(3):
            load(i, group).start()
    for k in range(chunks):
        own_outputs(k).start()
    pl.semaphore_wait(barrier, len(partners))
    for k in range(2):
        for way in range(2):
            direct(k, way).start()

    take_codes.wait()
    scales = scales_ref[own_rows(), :]
    blocks = scales.shape[1]
    block = chunks * span // blocks
    for b in range(blocks):
        k, at = divmod(b * block, span)
        spread = codes[:, b * block : (b + 1) * block].astype(jnp.float32)
        weight[k, 2 * z + c, :, at : at + block] = (spread * scales[:, b : b + 1]).astype(
            jnp.bfloat16
        )
    send_line(0)
    share(z).start()

    def forward_group(group, carry):
        level, a = group // 2, group % 2
        for i in range(3):
            load(i, group).wait()
        for head in range(heads):
            cols = slice(head * HD, (head + 1) * HD)
            prob = probs_t(ins[0, group, :, cols], ins[1, group, :, cols])
            prob = prob.astype(jnp.bfloat16)
            probs[group * heads + head] = prob
            made = dot(ins[2, group, :, cols], prob, ((0,), (0,))).astype(jnp.bfloat16)
            for core, rep, low, high, at in pieces[head]:
                outgoing[a, rep, level, core, low:high, :] = made[at : at + high - low]

        @pl.when(a == 1)
        def _():
            for i in (2, 0, 1):
                send_context(i, level).start()
            keep_context(level).start()

        return carry

    lax.fori_loop(0, groups, forward_group, 0)

    def weight_part(k, core):
        left = context[:, core].reshape(depth * slab, -1)
        right = near[k].reshape(-1, span)
        return dot(left, right, ((1,), (0,)))

    def grad_part(k, slot):
        left = weight[k].reshape(-1, span)
        return dot(left, near[k, slot], ((1,), (1,)))

    def grad_chunk(k, first):
        def body(slot, carry):
            part = grad_part(k, slot)
            total[slot] = part if first else total[slot] + part
            return carry

        lax.fori_loop(0, 4, body, 0)

    def take_direct(k):
        for way in range(2):
            direct(k, way).wait_recv()
            relay(k, way).start()

    def take_relayed(k):
        own_outputs(k).wait()
        for way in range(2):
            relay(k, way).wait_recv()

    def weight_chunk(k):
        made = weight_part(k, 1 - c).astype(jnp.bfloat16)
        part_out[k] = made.reshape(depth, slab, span)
        send_part(k).start()
        part[...] = weight_part(k, c).reshape(depth, slab, span)
        send_part(k).wait_recv()
        for level in range(depth):
            summed = part[level] + part_in[k, level].astype(jnp.float32)
            part[level] = summed
            sum_out[k, level] = summed.astype(jnp.bfloat16)
        own_sum[k] = part[z]
        for d in reversed(range(depth - 1)):
            send_sum(k, d).start()

    def grad_chunk(k, carry):
        def body(slot, inner):
            total[slot] = total[slot] + grad_part(k, slot)
            return inner

        return lax.fori_loop(0, 4, body, carry)

    receive_line(1)
    total[...] = jnp.zeros_like(total)
    ready = depth - 2

    def chunk(k, carry):
        take_direct(k)

        @pl.when(k + 2 < chunks)
        def _():
            for way in range(2):
                direct(k + 2, way).start()

        @pl.when(k == 0)
        def _():
            for level in range(depth):
                keep_context(level).wait()
                for i in range(3):
                    send_context(i, level).wait_recv()

        take_relayed(k)
        weight_chunk(k)
        for step in range(2, depth):
            pl.when(k == step - 2)(functools.partial(receive_line, step))

        @pl.when(k == ready)
        def _():
            for level in range(depth):
                share_in(level).wait_recv()
            lax.fori_loop(0, ready + 1, grad_chunk, 0)

        @pl.when(k > ready)
        def _():
            grad_chunk(k, 0)

        return carry

    lax.fori_loop(0, chunks - 1, chunk, 0)
    last = chunks - 1
    take_direct(last)
    take_relayed(last)
    for slot in (2, 3, 1, 0):
        made = (total[slot] + grad_part(last, slot)).astype(jnp.bfloat16)
        grads_out[slot] = made.reshape(depth, CORES, slab, seq)
        for level in range(depth):
            if slot:
                send_grad(slot - 1, level).start()
            else:
                keep_grad(level).start()
    weight_chunk(last)

    def backward_group(level, a):
        group = 2 * level + a
        for head in range(heads):
            cols = slice(head * HD, (head + 1) * HD)
            query, keyset = ins[0, group, :, cols], ins[1, group, :, cols]
            grad = [
                grads[a, rep, level, core, low:high, :]
                for core, rep, low, high, _ in pieces[head]
            ]
            grad = grad[0] if len(grad) == 1 else jnp.concatenate(grad, axis=0)
            prob = probs[group * heads + head]
            results[2, group, :, cols] = dot(prob, grad, ((1,), (1,))).astype(jnp.bfloat16)
            dprob = dot(ins[2, group, :, cols], grad, ((1,), (0,)))
            prob = prob.astype(jnp.float32)
            delta = jnp.sum(prob * dprob, axis=0, keepdims=True)
            dscore = (prob * (dprob - delta) * SCALE).astype(jnp.bfloat16)
            results[1, group, :, cols] = dot(dscore, query, ((1,), (0,))).astype(jnp.bfloat16)
            results[0, group, :, cols] = dot(dscore, keyset, ((0,), (0,))).astype(jnp.bfloat16)
        for i in range(3):
            store(i, group).start()

    def backward_near(level, carry):
        keep_grad(level).wait()
        grad_in(1, level).wait_recv()
        backward_group(level, x)
        return carry

    def backward_far(level, carry):
        grad_in(0, level).wait_recv()
        grad_in(2, level).wait_recv()
        backward_group(level, 1 - x)
        return carry

    def store_sum(k):
        columns = pl.ds(pl.multiple_of(k * span, span), span)
        return pltpu.make_async_copy(own_sum.at[k], dw_hbm.at[:, columns], dw_sem.at[k])

    def finish_sum(k, carry):
        summed = own_sum[k]
        for d in range(depth - 1):
            send_sum(k, d).wait_recv()
            summed = summed + sum_in[k, d].astype(jnp.float32)
        own_sum[k] = summed
        store_sum(k).start()
        return carry

    lax.fori_loop(0, depth, backward_near, 0)
    lax.fori_loop(0, chunks, finish_sum, 0)
    lax.fori_loop(0, depth, backward_far, 0)

    def drain_chunk(k, carry):
        for way in range(2):
            direct(k, way).wait_send()
            relay(k, way).wait_send()
        send_part(k).wait_send()
        for d in range(depth - 1):
            send_sum(k, d).wait_send()
        store_sum(k).wait()
        return carry

    def drain_level(level, carry):
        for i in range(3):
            send_context(i, level).wait_send()
            send_grad(i, level).wait_send()
        share(level).wait_send()
        return carry

    def drain_group(group, carry):
        for i in range(3):
            store(i, group).wait()
        return carry

    lax.fori_loop(0, chunks, drain_chunk, 0)
    lax.fori_loop(0, depth, drain_level, 0)
    for step in range(depth - 1):

        @pl.when((z - step >= 0) & (z + 1 < depth))
        def _():
            line(True, step).wait_send()

        @pl.when((z + step < depth) & (z - 1 >= 0))
        def _():
            line(False, step).wait_send()

    lax.fori_loop(0, groups, drain_group, 0)


def head_pieces(width, slab, reps):
    pieces = []
    for head in range(width // HD):
        at, end, found = head * HD, (head + 1) * HD, []
        while at < end:
            block, low = divmod(at, slab)
            count = min(slab - low, end - at)
            found.append((block // reps, block % reps, low, low + count, at - head * HD))
            at += count
        pieces.append(found)
    return pieces


def fits(extents, depth, images, seq, rows, features, blocks):
    if extents != (2, CORES, 2) or images != 1 or not 2 <= depth <= CHUNKS:
        return False
    slab, span = rows // (depth * 8), features // CHUNKS
    return (
        rows == depth * 8 * slab
        and slab % 16 == 0
        and (4 * slab) % HD == 0
        and features == CHUNKS * span
        and span % (features // blocks) == 0
        and (features // blocks) % 128 == 0
        and seq % 128 == 0
    )


def fused(queries, keys, values, grad_output, weight_codes, weight_scales):
    _, seq, rows = queries.shape
    features = grad_output.shape[-1]
    depth = lax.axis_size("z")
    slab, span = rows // (depth * 8), features // CHUNKS
    width = 4 * slab
    groups, heads = 2 * depth, width // HD
    half, whole = jnp.bfloat16, jnp.float32
    dma = pltpu.SemaphoreType.DMA
    anywhere = pl.BlockSpec(memory_space=pl.ANY)
    image = jax.ShapeDtypeStruct((seq, rows), half)
    scratch = [
        pltpu.VMEM((3, groups, seq, width), half),
        pltpu.VMEM((slab, features), half),
        pltpu.VMEM((CHUNKS, 4, seq, span), half),
        pltpu.VMEM((CHUNKS, 2 * depth, slab, span), half),
        pltpu.VMEM((depth, CORES, slab, 4 * seq), half),
        pltpu.VMEM((2, 2, depth, CORES, slab, seq), half),
        pltpu.VMEM((4, rows // 4, seq), whole),
        pltpu.VMEM((4, depth, CORES, slab, seq), half),
        pltpu.VMEM((2, 2, depth, CORES, slab, seq), half),
        pltpu.VMEM((CHUNKS, depth, slab, span), half),
        pltpu.VMEM((CHUNKS, depth, slab, span), half),
        pltpu.VMEM((CHUNKS, depth, slab, span), half),
        pltpu.VMEM((CHUNKS, depth - 1, slab, span), half),
        pltpu.VMEM((CHUNKS, slab, span), whole),
        pltpu.VMEM((depth, slab, span), whole),
        pltpu.VMEM((groups * heads, seq, seq), half),
        pltpu.VMEM((3, groups, seq, width), half),
        dma((3, groups)),
        dma,
        dma((CHUNKS,)),
        dma((2, CHUNKS)),
        dma((2, CHUNKS)),
        dma((2, CHUNKS)),
        dma((2, CHUNKS)),
        dma((3, depth)),
        dma((3, depth)),
        dma((depth,)),
        dma((2, depth - 1)),
        dma((2, depth - 1)),
        dma((depth,)),
        dma((depth,)),
        dma((CHUNKS,)),
        dma((CHUNKS,)),
        dma((CHUNKS, depth - 1)),
        dma((CHUNKS, depth - 1)),
        dma((3, depth)),
        dma((3, depth)),
        dma((depth,)),
        dma((3, groups)),
        dma((CHUNKS,)),
    ]
    *grads, total = pl.pallas_call(
        functools.partial(fused_kernel, depth, CHUNKS, head_pieces(width, slab, 2)),
        in_specs=[anywhere] * 5 + [pl.BlockSpec(memory_space=pltpu.VMEM)],
        out_specs=[anywhere] * 4,
        out_shape=[image] * 3 + [jax.ShapeDtypeStruct((slab, features), whole)],
        scratch_shapes=scratch,
        compiler_params=pltpu.CompilerParams(
            collective_id=0, has_side_effects=True, vmem_limit_bytes=60 << 20
        ),
        name="fused",
    )(queries[0], keys[0], values[0], grad_output[0], weight_codes, weight_scales)
    return (*(grad[None] for grad in grads), total)


def per_device(queries, keys, values, grad_output, weight_codes, weight_scales):
    image_count, seq, rows = queries.shape
    depth = lax.axis_size("z")
    extents = tuple(lax.axis_size(axis) for axis in PLANE)
    sizes = (image_count, seq, rows, grad_output.shape[-1], weight_scales.shape[-1])
    if fits(extents, depth, *sizes):
        return fused(queries, keys, values, grad_output, weight_codes, weight_scales)
    home = tuple(lax.axis_index(axis) for axis in PLANE)
    replicas, peers = extents[-1], math.prod(extents)
    slab = rows // (depth * peers)
    share = depth * slab
    steps = list(itertools.product(*(range(n) for n in extents)))

    def shifted(value, step):
        pairs = []
        for source, place in enumerate(steps):
            to = 0
            for at, move, n in zip(place, step, extents):
                to = to * n + (at + move) % n
            pairs.append((source, to))
        return lax.ppermute(value, PLANE, pairs)

    def start_at(step):
        return (0, *((h + s) % n for h, s, n in zip(home, step, extents)), 0, 0)

    own = home[-1] * slab
    codes = lax.dynamic_slice_in_dim(weight_codes, own, slab, 0)
    scales = lax.dynamic_slice_in_dim(weight_scales, own, slab, 0)
    weight = lax.all_gather(restore(codes, scales), "z", axis=0, tiled=True)

    kept = []
    for image in range(image_count):
        first = grad_output[image]
        straight = [shifted(first, (0, 0, r)) for r in range(1, replicas)]
        across = shifted(first, (1, 0, 0))
        context = forward(queries[image], keys[image], values[image])
        context = context.reshape(depth, *extents, slab, seq)
        pieces = [
            lax.dynamic_slice(context, start_at(step), (depth, 1, 1, 1, slab, seq)).reshape(
                share, seq
            )
            for step in steps
        ]
        contexts = [pieces[0]] + [shifted(p, step) for p, step in zip(pieces[1:], steps[1:])]
        across, straight, _ = lax.optimization_barrier((across, straight, pieces[0]))
        half = seq // 2
        corner = [
            jnp.concatenate(
                [shifted(piece[:half], (1, 0, 0)), shifted(across[half:], (0, 0, r))]
            )
            for r, piece in enumerate(straight, 1)
        ]
        near = {(0, 0): first, (1, 0): across}
        for r in range(1, replicas):
            near[0, r], near[1, r] = straight[r - 1], corner[r - 1]
        outputs = [
            near[x, r] if c == 0 else shifted(near[x, r], (0, 1, 0)) for x, c, r in steps
        ]
        kept.append((outputs, contexts))
    terms = weight_terms(
        [c for pair in kept for c in pair[1]], [o for pair in kept for o in pair[0]]
    )
    total = lax.psum_scatter(terms, "z", scatter_dimension=0, tiled=True)
    results = []
    for image in range(image_count):
        grad = jnp.zeros((depth, *extents, slab, seq), jnp.bfloat16)
        for step, output in zip(steps, kept[image][0]):
            piece = dot(weight, output, ((1,), (1,))).astype(jnp.bfloat16)
            if any(step):
                piece = shifted(piece, tuple(-s for s in step))
            grad = lax.dynamic_update_slice(
                grad, piece.reshape(depth, 1, 1, 1, slab, seq), start_at(step)
            )
        results.append(
            backward(queries[image], keys[image], values[image], grad.reshape(rows, seq))
        )
    grads = [
        parts[0][None] if image_count == 1 else jnp.stack(parts) for parts in zip(*results)
    ]
    return (*grads, total.astype(jnp.float32))


def solution(mesh):
    groups, replicas = mesh.shape["group"], mesh.shape["rep"]
    split = Mesh(
        mesh.devices.reshape(groups // (2 * CORES), 2, CORES, replicas), ("z", *PLANE)
    )
    images = P(("z", *PLANE), None, None)
    shards = P(("z", "x", "core"), None)
    return jax.shard_map(
        per_device,
        mesh=split,
        in_specs=(images,) * 4 + (shards,) * 2,
        out_specs=(images,) * 3 + (P(("z", *PLANE), None),),
        check_vma=False,
    )
```

```python
import functools
import itertools
import math

import jax
import jax.numpy as jnp
from jax import lax
from jax.experimental import pallas as pl
from jax.experimental.pallas import tpu as pltpu
from jax.sharding import Mesh, PartitionSpec as P

HD = 128
SCALE = HD ** (-0.5)
CORES = 2
PLANE = ("x", "core", "rep")


def dot(a, b, dims):
    return lax.dot_general(a, b, (dims, ((), ())), preferred_element_type=jnp.float32)


def probs_t(query, keyset):
    scores = dot(keyset, query, ((1,), (1,)))
    highest = jnp.max(scores, axis=0, keepdims=True)
    exponent = jnp.exp2((scores - highest) * (SCALE * math.log2(math.e)))
    return exponent * (1.0 / jnp.sum(exponent, axis=0, keepdims=True))


def forward_kernel(heads, q_ref, k_ref, v_ref, ctx_ref):
    for head in range(heads):
        cols = slice(head * HD, (head + 1) * HD)
        prob = probs_t(q_ref[:, cols], k_ref[:, cols]).astype(jnp.bfloat16)
        ctx_ref[cols, :] = dot(v_ref[:, cols], prob, ((0,), (0,))).astype(jnp.bfloat16)


def backward_kernel(heads, q_ref, k_ref, v_ref, g_ref, dq_ref, dk_ref, dv_ref):
    for head in range(heads):
        cols = slice(head * HD, (head + 1) * HD)
        query, keyset, grad = q_ref[:, cols], k_ref[:, cols], g_ref[cols, :]
        prob = probs_t(query, keyset)
        dv_ref[:, cols] = dot(prob.astype(jnp.bfloat16), grad, ((1,), (1,))).astype(jnp.bfloat16)
        dprob = dot(v_ref[:, cols], grad, ((1,), (0,)))
        delta = jnp.sum(prob * dprob, axis=0, keepdims=True)
        dscore = (prob * (dprob - delta) * SCALE).astype(jnp.bfloat16)
        dk_ref[:, cols] = dot(dscore, query, ((1,), (0,))).astype(jnp.bfloat16)
        dq_ref[:, cols] = dot(dscore, keyset, ((0,), (0,))).astype(jnp.bfloat16)


def heads_per_step(head_count):
    return next(n for n in (4, 3, 2, 1) if head_count % n == 0)


def forward(query, keyset, valueset):
    seq, rows = query.shape
    heads = heads_per_step(rows // HD)
    wide = pl.BlockSpec((seq, heads * HD), lambda i: (0, i))
    return pl.pallas_call(
        functools.partial(forward_kernel, heads),
        grid=(rows // (heads * HD),),
        in_specs=[wide] * 3,
        out_specs=pl.BlockSpec((heads * HD, seq), lambda i: (i, 0)),
        out_shape=jax.ShapeDtypeStruct((rows, seq), jnp.bfloat16),
        cost_estimate=pl.CostEstimate(
            flops=4 * seq * seq * rows,
            bytes_accessed=8 * seq * rows,
            transcendentals=seq * seq * rows // HD,
        ),
        name="forward",
    )(query, keyset, valueset)


def backward(query, keyset, valueset, grad_t):
    seq, rows = query.shape
    heads = heads_per_step(rows // HD)
    wide = pl.BlockSpec((seq, heads * HD), lambda i: (0, i))
    return pl.pallas_call(
        functools.partial(backward_kernel, heads),
        grid=(rows // (heads * HD),),
        in_specs=[wide] * 3 + [pl.BlockSpec((heads * HD, seq), lambda i: (i, 0))],
        out_specs=[wide] * 3,
        out_shape=[jax.ShapeDtypeStruct((seq, rows), jnp.bfloat16)] * 3,
        cost_estimate=pl.CostEstimate(
            flops=10 * seq * seq * rows,
            bytes_accessed=14 * seq * rows,
            transcendentals=seq * seq * rows // HD,
        ),
        name="backward",
    )(query, keyset, valueset, grad_t)


def term_kernel(count, *refs):
    total = None
    for i in range(count):
        part = dot(refs[i][...], refs[count + i][...], ((1,), (0,)))
        total = part if total is None else total + part
    refs[-1][...] = total.astype(jnp.bfloat16)


def weight_terms(contexts, outputs):
    count = len(contexts)
    rows, seq = contexts[0].shape
    features = outputs[0].shape[1]
    tile = math.gcd(features, 512)
    return pl.pallas_call(
        functools.partial(term_kernel, count),
        grid=(features // tile,),
        in_specs=[pl.BlockSpec((rows, seq), lambda i: (0, 0))] * count
        + [pl.BlockSpec((seq, tile), lambda i: (0, i))] * count,
        out_specs=pl.BlockSpec((rows, tile), lambda i: (0, i)),
        out_shape=jax.ShapeDtypeStruct((rows, features), jnp.bfloat16),
        cost_estimate=pl.CostEstimate(
            flops=2 * rows * seq * features * count,
            bytes_accessed=2 * (count * seq * (rows + features) + rows * features),
            transcendentals=0,
        ),
        name="terms",
    )(*contexts, *outputs)


def restore(codes, scales):
    rows, blocks = scales.shape
    spread = codes.astype(jnp.float32).reshape(rows, blocks, -1) * scales[:, :, None]
    return spread.reshape(rows, -1).astype(jnp.bfloat16)


MESH_ID = pl.DeviceIdType.MESH
AXES = ("z", "x", "core", "rep")
CHUNKS = 6


def fused_kernel(
    depth,
    chunks,
    pieces,
    q_hbm,
    k_hbm,
    v_hbm,
    g_hbm,
    codes_hbm,
    scales_hbm,
    dq_ref,
    dk_ref,
    dv_ref,
    dw_ref,
    ins,
    codes,
    scales_in,
    scales_ref,
    near,
    weight,
    context,
    outgoing,
    total,
    grads_out,
    grads,
    part_out,
    part_in,
    pair_out,
    pair_in,
    far_sum,
    far_out,
    far_in,
    own_sum,
    part,
    probs,
    in_sem,
    codes_sem,
    scales_sem,
    own_sem,
    direct_send,
    direct_recv,
    relay_send,
    relay_recv,
    ctx_send,
    ctx_recv,
    ctx_own,
    line_send,
    line_recv,
    sib_send,
    sib_recv,
    part_send,
    part_recv,
    pair_send,
    pair_recv,
    far_send,
    far_recv,
    grad_send,
    grad_recv,
    grad_own,
):
    z, x, c, y = (lax.axis_index(axis) for axis in AXES)
    groups, seq, width = ins.shape[1:]
    heads = width // HD
    slab = codes.shape[0]
    span = near.shape[-1]
    half = seq // 2
    across, along, corner = (z, 1 - x, c, y), (z, x, c, 1 - y), (z, 1 - x, c, 1 - y)
    sibling = (z, x, 1 - c, y)
    plane = (across, along, corner)
    owners = ((1 - x, y), (x, 1 - y), (1 - x, 1 - y))
    mate, far = z + 1 - 2 * (z % 2), (z + 2) % depth
    mate_far = (mate + 2) % depth
    middle = (z % 2 - z // 2) * (z % 2 - z // 2)

    barrier = pltpu.get_barrier_semaphore()
    partners = [*plane, sibling, (mate, x, c, y), (far, x, c, y)]
    for partner in partners:
        pl.semaphore_signal(barrier, inc=1, device_id=partner, device_id_type=MESH_ID)

    @pl.when(middle == 1)
    def _():
        other = (depth - 1 - z, x, c, y)
        pl.semaphore_signal(barrier, inc=1, device_id=other, device_id_type=MESH_ID)

    def remote(source, target, send, recv, device):
        return pltpu.make_async_remote_copy(
            src_ref=source,
            dst_ref=target,
            send_sem=send,
            recv_sem=recv,
            device_id=device,
            device_id_type=MESH_ID,
        )

    def own_rows():
        return pl.ds(pl.multiple_of(y * slab, slab), slab)

    def load(i, group):
        source = (q_hbm, k_hbm, v_hbm)[i]
        columns = pl.ds(pl.multiple_of(group * width, width), width)
        return pltpu.make_async_copy(
            source.at[:, columns], ins.at[i, group], in_sem.at[i, group]
        )

    def own_outputs(k):
        columns = pl.ds(pl.multiple_of(k * span, span), span)
        return pltpu.make_async_copy(g_hbm.at[:, columns], near.at[k, 0], own_sem.at[k])

    def direct(k, way):
        columns = pl.ds(pl.multiple_of(k * span, span), span)
        return remote(
            g_hbm.at[:, columns],
            near.at[k, 1 + way],
            direct_send.at[way, k],
            direct_recv.at[way, k],
            plane[way],
        )

    def relay(k, way):
        rows = pl.ds(way * half, half)
        return remote(
            near.at[k, 1 + way, rows],
            near.at[k, 3, rows],
            relay_send.at[way, k],
            relay_recv.at[way, k],
            plane[1 - way],
        )

    def send_context(i, level):
        a, b = owners[i]
        return remote(
            outgoing.at[a, b, level],
            context.at[level, :, :, pl.ds((1 + i) * seq, seq)],
            ctx_send.at[i, level],
            ctx_recv.at[i, level],
            plane[i],
        )

    def keep_context(level):
        return pltpu.make_async_copy(
            outgoing.at[x, y, level],
            context.at[level, :, :, pl.ds(0, seq)],
            ctx_own.at[level],
        )

    def line(up, step):
        block = z - step if up else z + step
        at = weight.at[:, 2 * block + c]
        way = 0 if up else 1
        target = (z + 1 if up else z - 1, x, c, y)
        return remote(at, at, line_send.at[way, step], line_recv.at[way, step], target)

    def line_in(up, step):
        block = z - step if up else z + step
        at = weight.at[:, 2 * block + c]
        way = 0 if up else 1
        target = (z + 1 if up else z - 1, x, c, y)
        return remote(
            at, at, line_send.at[way, step - 1], line_recv.at[way, step - 1], target
        )

    def share(block):
        at = weight.at[:, 2 * block + c]
        return remote(at, at, sib_send.at[block], sib_recv.at[block], sibling)

    def share_in(block):
        at = weight.at[:, 2 * block + 1 - c]
        return remote(at, at, sib_send.at[block], sib_recv.at[block], sibling)

    def send_line(step):
        if step < depth - 1:

            @pl.when((z - step >= 0) & (z + 1 < depth))
            def _():
                line(True, step).start()

            @pl.when((z + step < depth) & (z - 1 >= 0))
            def _():
                line(False, step).start()

    def receive_line(step):
        @pl.when(z - step >= 0)
        def _():
            line_in(True, step).wait_recv()

        @pl.when(z + step < depth)
        def _():
            line_in(False, step).wait_recv()

        send_line(step)

        @pl.when(z - step >= 0)
        def _():
            share(z - step).start()

        @pl.when(z + step < depth)
        def _():
            share(z + step).start()

    def send_part(k):
        return remote(
            part_out.at[k], part_in.at[k], part_send.at[k], part_recv.at[k], sibling
        )

    def send_pair(k):
        return remote(
            pair_out.at[k],
            pair_in.at[k],
            pair_send.at[k],
            pair_recv.at[k],
            (mate, x, c, y),
        )

    def send_far(k):
        return remote(
            far_out.at[k], far_in.at[k], far_send.at[k], far_recv.at[k], (far, x, c, y)
        )

    def send_grad(i, level):
        return remote(
            grads_out.at[1 + i, level],
            grads.at[x, y, level],
            grad_send.at[i, level],
            grad_recv.at[i, level],
            plane[i],
        )

    def grad_in(i, level):
        a, b = owners[i]
        return remote(
            grads_out.at[1 + i, level],
            grads.at[a, b, level],
            grad_send.at[i, level],
            grad_recv.at[i, level],
            plane[i],
        )

    def keep_grad(level):
        return pltpu.make_async_copy(
            grads_out.at[0, level], grads.at[x, y, level], grad_own.at[level]
        )

    take_codes = pltpu.make_async_copy(codes_hbm.at[own_rows()], codes, codes_sem)
    take_scales = pltpu.make_async_copy(scales_hbm, scales_in, scales_sem)
    take_codes.start()
    take_scales.start()
    for group in range(groups):
        for i in range(3):
            load(i, group).start()
    for k in range(chunks):
        own_outputs(k).start()
    pl.semaphore_wait(barrier, len(partners) + middle)
    for k in range(2):
        for way in range(2):
            direct(k, way).start()

    take_codes.wait()
    take_scales.wait()
    scales_ref[...] = scales_in[...].T
    scales = scales_ref[own_rows(), :]
    blocks = scales.shape[1]
    block = chunks * span // blocks
    for b in range(blocks):
        k, at = divmod(b * block, span)
        spread = codes[:, b * block : (b + 1) * block].astype(jnp.float32)
        weight[k, 2 * z + c, :, at : at + block] = (spread * scales[:, b : b + 1]).astype(
            jnp.bfloat16
        )
    send_line(0)
    share(z).start()

    def forward_group(group, carry):
        level, a = group // 2, group % 2
        for i in range(3):
            load(i, group).wait()
        for head in range(heads):
            cols = slice(head * HD, (head + 1) * HD)
            prob = probs_t(ins[0, group, :, cols], ins[1, group, :, cols])
            prob = prob.astype(jnp.bfloat16)
            probs[group * heads + head] = prob
            made = dot(ins[2, group, :, cols], prob, ((0,), (0,))).astype(jnp.bfloat16)
            for core, rep, low, high, at in pieces[head]:
                outgoing[a, rep, level, core, low:high, :] = made[at : at + high - low]

        @pl.when(a == 1)
        def _():
            for i in (2, 0, 1):
                send_context(i, level).start()
            keep_context(level).start()

        return carry

    lax.fori_loop(0, groups, forward_group, 0)

    def weight_part(k, core):
        left = context[:, core].reshape(depth * slab, -1)
        right = near[k].reshape(-1, span)
        return dot(left, right, ((1,), (0,)))

    def grad_part(k, slot):
        left = weight[k].reshape(-1, span)
        return dot(left, near[k, slot], ((1,), (1,)))

    def grad_chunk(k, first):
        def body(slot, carry):
            part = grad_part(k, slot)
            total[slot] = part if first else total[slot] + part
            return carry

        lax.fori_loop(0, 4, body, 0)

    def start_direct(k):
        for way in range(2):
            direct(k, way).start()

    def take_direct(k):
        for way in range(2):
            direct(k, way).wait_recv()
            relay(k, way).start()

    def take_relayed(k):
        own_outputs(k).wait()
        for way in range(2):
            relay(k, way).wait_recv()

    def start_part(k):
        made = weight_part(k, 1 - c).astype(jnp.bfloat16)
        part_out[k] = made.reshape(depth, slab, span)
        send_part(k).start()
        part[...] = weight_part(k, c).reshape(depth, slab, span)

    def finish_part(k):
        send_part(k).wait_recv()

        def summed(level):
            return part[level] + part_in[k, level].astype(jnp.float32)

        pair_out[k, 1] = summed(mate_far).astype(jnp.bfloat16)
        pair_out[k, 0] = summed(mate).astype(jnp.bfloat16)
        send_pair(k).start()
        far_sum[...] = summed(far)
        own_sum[k] = summed(z)

    def pass_far(k):
        send_pair(k).wait_recv()
        far_out[k] = (far_sum[...] + pair_in[k, 1].astype(jnp.float32)).astype(jnp.bfloat16)
        send_far(k).start()

    def grad_chunk(k, carry):
        def body(slot, inner):
            total[slot] = total[slot] + grad_part(k, slot)
            return inner

        return lax.fori_loop(0, 4, body, carry)

    def end_grad(slot):
        made = (total[slot] + grad_part(last, slot)).astype(jnp.bfloat16)
        grads_out[slot] = made.reshape(depth, CORES, slab, seq)
        for level in range(depth):
            if slot:
                send_grad(slot - 1, level).start()
            else:
                keep_grad(level).start()

    total[...] = jnp.zeros_like(total)
    last, ready = chunks - 1, 2
    receive_line(1)
    take_direct(0)
    start_direct(2)
    receive_line(2)
    for level in range(depth):
        keep_context(level).wait()
        for i in range(3):
            send_context(i, level).wait_recv()

    def chunk(k, carry):
        take_relayed(k)
        take_direct(k + 1)

        @pl.when(k + 3 < chunks)
        def _():
            start_direct(k + 3)

        start_part(k)

        @pl.when(k > 0)
        def _():
            pass_far(k - 1)

        @pl.when(k == ready - 1)
        def _():
            for step in range(3, depth):
                receive_line(step)

        @pl.when(k == ready)
        def _():
            for level in range(depth):
                share_in(level).wait_recv()

        @pl.when(k >= ready)
        def _():
            low = 2 * (k - ready)
            lax.fori_loop(low, low + 2 - k // (last - 1), grad_chunk, 0)

        finish_part(k)
        return carry

    lax.fori_loop(0, last, chunk, 0)
    end_grad(2)
    end_grad(1)
    own_outputs(last).wait()
    end_grad(0)
    for way in range(2):
        relay(last, way).wait_recv()
    end_grad(3)
    start_part(last)
    pass_far(last - 1)
    finish_part(last)

    def backward_group(level, a):
        group = 2 * level + a
        for head in range(heads):
            cols = slice(head * HD, (head + 1) * HD)
            query, keyset = ins[0, group, :, cols], ins[1, group, :, cols]
            grad = [
                grads[a, rep, level, core, low:high, :]
                for core, rep, low, high, _ in pieces[head]
            ]
            grad = grad[0] if len(grad) == 1 else jnp.concatenate(grad, axis=0)
            prob = probs[group * heads + head]
            into = pl.ds(pl.multiple_of(group * width + head * HD, HD), HD)
            dv_ref[:, into] = dot(prob, grad, ((1,), (1,))).astype(jnp.bfloat16)
            dprob = dot(ins[2, group, :, cols], grad, ((1,), (0,)))
            prob = prob.astype(jnp.float32)
            delta = jnp.sum(prob * dprob, axis=0, keepdims=True)
            dscore = (prob * (dprob - delta) * SCALE).astype(jnp.bfloat16)
            dk_ref[:, into] = dot(dscore, query, ((1,), (0,))).astype(jnp.bfloat16)
            dq_ref[:, into] = dot(dscore, keyset, ((0,), (0,))).astype(jnp.bfloat16)

    def backward_near(level, carry):
        keep_grad(level).wait()
        grad_in(1, level).wait_recv()
        backward_group(level, x)
        return carry

    def backward_far(level, carry):
        grad_in(0, level).wait_recv()
        grad_in(2, level).wait_recv()
        backward_group(level, 1 - x)
        return carry

    def finish_sum(k, carry):
        send_far(k).wait_recv()
        columns = pl.ds(pl.multiple_of(k * span, span), span)
        both = pair_in[k, 0].astype(jnp.float32) + far_in[k].astype(jnp.float32)
        dw_ref[:, columns] = own_sum[k] + both
        return carry

    backward_near(0, 0)
    pass_far(last)
    lax.fori_loop(1, depth, backward_near, 0)
    lax.fori_loop(0, chunks, finish_sum, 0)
    lax.fori_loop(0, depth, backward_far, 0)

    def drain_chunk(k, carry):
        for way in range(2):
            direct(k, way).wait_send()
            relay(k, way).wait_send()
        send_part(k).wait_send()
        send_pair(k).wait_send()
        send_far(k).wait_send()
        return carry

    def drain_level(level, carry):
        for i in range(3):
            send_context(i, level).wait_send()
            send_grad(i, level).wait_send()
        share(level).wait_send()
        return carry

    lax.fori_loop(0, chunks, drain_chunk, 0)
    lax.fori_loop(0, depth, drain_level, 0)
    for step in range(depth - 1):

        @pl.when((z - step >= 0) & (z + 1 < depth))
        def _():
            line(True, step).wait_send()

        @pl.when((z + step < depth) & (z - 1 >= 0))
        def _():
            line(False, step).wait_send()


def head_pieces(width, slab, reps):
    pieces = []
    for head in range(width // HD):
        at, end, found = head * HD, (head + 1) * HD, []
        while at < end:
            block, low = divmod(at, slab)
            count = min(slab - low, end - at)
            found.append((block // reps, block % reps, low, low + count, at - head * HD))
            at += count
        pieces.append(found)
    return pieces


def fits(extents, depth, images, seq, rows, features, blocks):
    if extents != (2, CORES, 2) or images != 1 or depth != 4:
        return False
    slab, span = rows // (depth * 8), features // CHUNKS
    return (
        rows == depth * 8 * slab
        and slab % 16 == 0
        and (4 * slab) % HD == 0
        and features == CHUNKS * span
        and span % (features // blocks) == 0
        and (features // blocks) % 128 == 0
        and seq % 128 == 0
    )


def fused(queries, keys, values, grad_output, weight_codes, weight_scales):
    _, seq, rows = queries.shape
    features = grad_output.shape[-1]
    depth = lax.axis_size("z")
    slab, span = rows // (depth * 8), features // CHUNKS
    width = 4 * slab
    groups, heads = 2 * depth, width // HD
    half, whole = jnp.bfloat16, jnp.float32
    dma = pltpu.SemaphoreType.DMA
    anywhere = pl.BlockSpec(memory_space=pl.ANY)
    blocks = weight_scales.shape[-1]
    image = pltpu.VMEM((seq, rows), half)
    scratch = [
        pltpu.VMEM((3, groups, seq, width), half),
        pltpu.VMEM((slab, features), half),
        pltpu.VMEM((blocks, 2 * slab), whole),
        pltpu.VMEM((2 * slab, blocks), whole),
        pltpu.VMEM((CHUNKS, 4, seq, span), half),
        pltpu.VMEM((CHUNKS, 2 * depth, slab, span), half),
        pltpu.VMEM((depth, CORES, slab, 4 * seq), half),
        pltpu.VMEM((2, 2, depth, CORES, slab, seq), half),
        pltpu.VMEM((4, rows // 4, seq), whole),
        pltpu.VMEM((4, depth, CORES, slab, seq), half),
        pltpu.VMEM((2, 2, depth, CORES, slab, seq), half),
        pltpu.VMEM((CHUNKS, depth, slab, span), half),
        pltpu.VMEM((CHUNKS, depth, slab, span), half),
        pltpu.VMEM((CHUNKS, 2, slab, span), half),
        pltpu.VMEM((CHUNKS, 2, slab, span), half),
        pltpu.VMEM((slab, span), whole),
        pltpu.VMEM((CHUNKS, slab, span), half),
        pltpu.VMEM((CHUNKS, slab, span), half),
        pltpu.VMEM((CHUNKS, slab, span), whole),
        pltpu.VMEM((depth, slab, span), whole),
        pltpu.VMEM((groups * heads, seq, seq), half),
        dma((3, groups)),
        dma,
        dma,
        dma((CHUNKS,)),
        dma((2, CHUNKS)),
        dma((2, CHUNKS)),
        dma((2, CHUNKS)),
        dma((2, CHUNKS)),
        dma((3, depth)),
        dma((3, depth)),
        dma((depth,)),
        dma((2, depth - 1)),
        dma((2, depth - 1)),
        dma((depth,)),
        dma((depth,)),
        dma((CHUNKS,)),
        dma((CHUNKS,)),
        dma((CHUNKS,)),
        dma((CHUNKS,)),
        dma((CHUNKS,)),
        dma((CHUNKS,)),
        dma((3, depth)),
        dma((3, depth)),
        dma((depth,)),
    ]
    *grads, total = pl.pallas_call(
        functools.partial(fused_kernel, depth, CHUNKS, head_pieces(width, slab, 2)),
        in_specs=[anywhere] * 6,
        out_specs=[pl.BlockSpec(memory_space=pltpu.VMEM)] * 4,
        out_shape=[image] * 3 + [pltpu.VMEM((slab, features), whole)],
        scratch_shapes=scratch,
        compiler_params=pltpu.CompilerParams(
            collective_id=0, has_side_effects=True, vmem_limit_bytes=48 << 20
        ),
        name="fused",
    )(queries[0], keys[0], values[0], grad_output[0], weight_codes, weight_scales.T)
    return (*(grad[None] for grad in grads), total)


def per_device(queries, keys, values, grad_output, weight_codes, weight_scales):
    image_count, seq, rows = queries.shape
    depth = lax.axis_size("z")
    extents = tuple(lax.axis_size(axis) for axis in PLANE)
    sizes = (image_count, seq, rows, grad_output.shape[-1], weight_scales.shape[-1])
    if fits(extents, depth, *sizes):
        return fused(queries, keys, values, grad_output, weight_codes, weight_scales)
    home = tuple(lax.axis_index(axis) for axis in PLANE)
    replicas, peers = extents[-1], math.prod(extents)
    slab = rows // (depth * peers)
    share = depth * slab
    steps = list(itertools.product(*(range(n) for n in extents)))

    def shifted(value, step):
        pairs = []
        for source, place in enumerate(steps):
            to = 0
            for at, move, n in zip(place, step, extents):
                to = to * n + (at + move) % n
            pairs.append((source, to))
        return lax.ppermute(value, PLANE, pairs)

    def start_at(step):
        return (0, *((h + s) % n for h, s, n in zip(home, step, extents)), 0, 0)

    own = home[-1] * slab
    codes = lax.dynamic_slice_in_dim(weight_codes, own, slab, 0)
    scales = lax.dynamic_slice_in_dim(weight_scales, own, slab, 0)
    weight = lax.all_gather(restore(codes, scales), "z", axis=0, tiled=True)

    kept = []
    for image in range(image_count):
        first = grad_output[image]
        straight = [shifted(first, (0, 0, r)) for r in range(1, replicas)]
        across = shifted(first, (1, 0, 0))
        context = forward(queries[image], keys[image], values[image])
        context = context.reshape(depth, *extents, slab, seq)
        pieces = [
            lax.dynamic_slice(context, start_at(step), (depth, 1, 1, 1, slab, seq)).reshape(
                share, seq
            )
            for step in steps
        ]
        contexts = [pieces[0]] + [shifted(p, step) for p, step in zip(pieces[1:], steps[1:])]
        across, straight, _ = lax.optimization_barrier((across, straight, pieces[0]))
        half = seq // 2
        corner = [
            jnp.concatenate(
                [shifted(piece[:half], (1, 0, 0)), shifted(across[half:], (0, 0, r))]
            )
            for r, piece in enumerate(straight, 1)
        ]
        near = {(0, 0): first, (1, 0): across}
        for r in range(1, replicas):
            near[0, r], near[1, r] = straight[r - 1], corner[r - 1]
        outputs = [
            near[x, r] if c == 0 else shifted(near[x, r], (0, 1, 0)) for x, c, r in steps
        ]
        kept.append((outputs, contexts))
    terms = weight_terms(
        [c for pair in kept for c in pair[1]], [o for pair in kept for o in pair[0]]
    )
    total = lax.psum_scatter(terms, "z", scatter_dimension=0, tiled=True)
    results = []
    for image in range(image_count):
        grad = jnp.zeros((depth, *extents, slab, seq), jnp.bfloat16)
        for step, output in zip(steps, kept[image][0]):
            piece = dot(weight, output, ((1,), (1,))).astype(jnp.bfloat16)
            if any(step):
                piece = shifted(piece, tuple(-s for s in step))
            grad = lax.dynamic_update_slice(
                grad, piece.reshape(depth, 1, 1, 1, slab, seq), start_at(step)
            )
        results.append(
            backward(queries[image], keys[image], values[image], grad.reshape(rows, seq))
        )
    grads = [
        parts[0][None] if image_count == 1 else jnp.stack(parts) for parts in zip(*results)
    ]
    return (*grads, total.astype(jnp.float32))


def solution(mesh):
    groups, replicas = mesh.shape["group"], mesh.shape["rep"]
    split = Mesh(
        mesh.devices.reshape(groups // (2 * CORES), 2, CORES, replicas), ("z", *PLANE)
    )
    images = P(("z", *PLANE), None, None)
    shards = P(("z", "x", "core"), None)
    return jax.shard_map(
        per_device,
        mesh=split,
        in_specs=(images,) * 4 + (shards,) * 2,
        out_specs=(images,) * 3 + (P(("z", *PLANE), None),),
        check_vma=False,
    )
```

```python
import functools
import itertools
import math

import jax
import jax.numpy as jnp
from jax import lax
from jax.experimental import pallas as pl
from jax.experimental.pallas import tpu as pltpu
from jax.sharding import Mesh, PartitionSpec as P

HD = 128
SCALE = HD ** (-0.5)
CORES = 2
PLANE = ("x", "core", "rep")


def dot(a, b, dims):
    return lax.dot_general(a, b, (dims, ((), ())), preferred_element_type=jnp.float32)


def probs_t(query, keyset):
    scores = dot(keyset, query, ((1,), (1,)))
    highest = jnp.max(scores, axis=0, keepdims=True)
    exponent = jnp.exp2((scores - highest) * (SCALE * math.log2(math.e)))
    return exponent * (1.0 / jnp.sum(exponent, axis=0, keepdims=True))


def forward_kernel(heads, q_ref, k_ref, v_ref, ctx_ref):
    for head in range(heads):
        cols = slice(head * HD, (head + 1) * HD)
        prob = probs_t(q_ref[:, cols], k_ref[:, cols]).astype(jnp.bfloat16)
        ctx_ref[cols, :] = dot(v_ref[:, cols], prob, ((0,), (0,))).astype(jnp.bfloat16)


def backward_kernel(heads, q_ref, k_ref, v_ref, g_ref, dq_ref, dk_ref, dv_ref):
    for head in range(heads):
        cols = slice(head * HD, (head + 1) * HD)
        query, keyset, grad = q_ref[:, cols], k_ref[:, cols], g_ref[cols, :]
        prob = probs_t(query, keyset)
        dv_ref[:, cols] = dot(prob.astype(jnp.bfloat16), grad, ((1,), (1,))).astype(jnp.bfloat16)
        dprob = dot(v_ref[:, cols], grad, ((1,), (0,)))
        delta = jnp.sum(prob * dprob, axis=0, keepdims=True)
        dscore = (prob * (dprob - delta) * SCALE).astype(jnp.bfloat16)
        dk_ref[:, cols] = dot(dscore, query, ((1,), (0,))).astype(jnp.bfloat16)
        dq_ref[:, cols] = dot(dscore, keyset, ((0,), (0,))).astype(jnp.bfloat16)


def heads_per_step(head_count):
    return next(n for n in (4, 3, 2, 1) if head_count % n == 0)


def forward(query, keyset, valueset):
    seq, rows = query.shape
    heads = heads_per_step(rows // HD)
    wide = pl.BlockSpec((seq, heads * HD), lambda i: (0, i))
    return pl.pallas_call(
        functools.partial(forward_kernel, heads),
        grid=(rows // (heads * HD),),
        in_specs=[wide] * 3,
        out_specs=pl.BlockSpec((heads * HD, seq), lambda i: (i, 0)),
        out_shape=jax.ShapeDtypeStruct((rows, seq), jnp.bfloat16),
        cost_estimate=pl.CostEstimate(
            flops=4 * seq * seq * rows,
            bytes_accessed=8 * seq * rows,
            transcendentals=seq * seq * rows // HD,
        ),
        name="forward",
    )(query, keyset, valueset)


def backward(query, keyset, valueset, grad_t):
    seq, rows = query.shape
    heads = heads_per_step(rows // HD)
    wide = pl.BlockSpec((seq, heads * HD), lambda i: (0, i))
    return pl.pallas_call(
        functools.partial(backward_kernel, heads),
        grid=(rows // (heads * HD),),
        in_specs=[wide] * 3 + [pl.BlockSpec((heads * HD, seq), lambda i: (i, 0))],
        out_specs=[wide] * 3,
        out_shape=[jax.ShapeDtypeStruct((seq, rows), jnp.bfloat16)] * 3,
        cost_estimate=pl.CostEstimate(
            flops=10 * seq * seq * rows,
            bytes_accessed=14 * seq * rows,
            transcendentals=seq * seq * rows // HD,
        ),
        name="backward",
    )(query, keyset, valueset, grad_t)


def term_kernel(count, *refs):
    total = None
    for i in range(count):
        part = dot(refs[i][...], refs[count + i][...], ((1,), (0,)))
        total = part if total is None else total + part
    refs[-1][...] = total.astype(jnp.bfloat16)


def weight_terms(contexts, outputs):
    count = len(contexts)
    rows, seq = contexts[0].shape
    features = outputs[0].shape[1]
    tile = math.gcd(features, 512)
    return pl.pallas_call(
        functools.partial(term_kernel, count),
        grid=(features // tile,),
        in_specs=[pl.BlockSpec((rows, seq), lambda i: (0, 0))] * count
        + [pl.BlockSpec((seq, tile), lambda i: (0, i))] * count,
        out_specs=pl.BlockSpec((rows, tile), lambda i: (0, i)),
        out_shape=jax.ShapeDtypeStruct((rows, features), jnp.bfloat16),
        cost_estimate=pl.CostEstimate(
            flops=2 * rows * seq * features * count,
            bytes_accessed=2 * (count * seq * (rows + features) + rows * features),
            transcendentals=0,
        ),
        name="terms",
    )(*contexts, *outputs)


def restore(codes, scales):
    rows, blocks = scales.shape
    spread = codes.astype(jnp.float32).reshape(rows, blocks, -1) * scales[:, :, None]
    return spread.reshape(rows, -1).astype(jnp.bfloat16)


MESH_ID = pl.DeviceIdType.MESH
AXES = ("z", "x", "core", "rep")
CHUNKS = 6


def fused_kernel(
    depth,
    chunks,
    pieces,
    q_hbm,
    k_hbm,
    v_hbm,
    g_hbm,
    codes_hbm,
    scales_hbm,
    dq_ref,
    dk_ref,
    dv_ref,
    dw_ref,
    ins,
    codes,
    scales_in,
    scales_ref,
    near,
    weight,
    context,
    outgoing,
    total,
    grads_out,
    grads,
    part_out,
    part_in,
    pair_out,
    pair_in,
    far_sum,
    far_out,
    far_in,
    own_sum,
    part,
    probs,
    in_sem,
    codes_sem,
    scales_sem,
    own_sem,
    direct_send,
    direct_recv,
    relay_send,
    relay_recv,
    ctx_send,
    ctx_recv,
    ctx_own,
    line_send,
    line_recv,
    sib_send,
    sib_recv,
    part_send,
    part_recv,
    pair_send,
    pair_recv,
    far_send,
    far_recv,
    grad_send,
    grad_recv,
    grad_own,
):
    z, x, c, y = (lax.axis_index(axis) for axis in AXES)
    groups, seq, width = ins.shape[1:]
    heads = width // HD
    slab = codes.shape[0]
    span = near.shape[-1]
    half = seq // 2
    across, along, corner = (z, 1 - x, c, y), (z, x, c, 1 - y), (z, 1 - x, c, 1 - y)
    sibling = (z, x, 1 - c, y)
    plane = (across, along, corner)
    owners = ((1 - x, y), (x, 1 - y), (1 - x, 1 - y))
    mate, far = z + 1 - 2 * (z % 2), (z + 2) % depth
    middle = (z % 2 - z // 2) * (z % 2 - z // 2)
    remote_levels = (2 - z // 2, (depth - 1) * (1 - z // 2))

    barrier = pltpu.get_barrier_semaphore()
    partners = [*plane, sibling, (mate, x, c, y), (far, x, c, y)]
    for partner in partners:
        pl.semaphore_signal(barrier, inc=1, device_id=partner, device_id_type=MESH_ID)

    @pl.when(middle == 1)
    def _():
        other = (depth - 1 - z, x, c, y)
        pl.semaphore_signal(barrier, inc=1, device_id=other, device_id_type=MESH_ID)

    def remote(source, target, send, recv, device):
        return pltpu.make_async_remote_copy(
            src_ref=source,
            dst_ref=target,
            send_sem=send,
            recv_sem=recv,
            device_id=device,
            device_id_type=MESH_ID,
        )

    def own_rows():
        return pl.ds(pl.multiple_of(y * slab, slab), slab)

    def load(i, group):
        source = (q_hbm, k_hbm, v_hbm)[i]
        columns = pl.ds(pl.multiple_of(group * width, width), width)
        return pltpu.make_async_copy(
            source.at[:, columns], ins.at[i, group], in_sem.at[i, group]
        )

    def own_outputs(k):
        columns = pl.ds(pl.multiple_of(k * span, span), span)
        return pltpu.make_async_copy(g_hbm.at[:, columns], near.at[k, 0], own_sem.at[k])

    def direct(k, way):
        columns = pl.ds(pl.multiple_of(k * span, span), span)
        return remote(
            g_hbm.at[:, columns],
            near.at[k, 1 + way],
            direct_send.at[way, k],
            direct_recv.at[way, k],
            plane[way],
        )

    def relay(k, way):
        rows = pl.ds(way * half, half)
        return remote(
            near.at[k, 1 + way, rows],
            near.at[k, 3, rows],
            relay_send.at[way, k],
            relay_recv.at[way, k],
            plane[1 - way],
        )

    def send_context(i, level):
        a, b = owners[i]
        return remote(
            outgoing.at[a, b, level],
            context.at[level, :, :, pl.ds((1 + i) * seq, seq)],
            ctx_send.at[i, level],
            ctx_recv.at[i, level],
            plane[i],
        )

    def keep_context(level):
        return pltpu.make_async_copy(
            outgoing.at[x, y, level],
            context.at[level, :, :, pl.ds(0, seq)],
            ctx_own.at[level],
        )

    def line(up, step):
        block = z - step if up else z + step
        at = weight.at[:, 2 * block + c]
        way = 0 if up else 1
        target = (z + 1 if up else z - 1, x, c, y)
        return remote(at, at, line_send.at[way, step], line_recv.at[way, step], target)

    def line_in(up, step):
        block = z - step if up else z + step
        at = weight.at[:, 2 * block + c]
        way = 0 if up else 1
        target = (z + 1 if up else z - 1, x, c, y)
        return remote(
            at, at, line_send.at[way, step - 1], line_recv.at[way, step - 1], target
        )

    def share(block):
        at = weight.at[:, 2 * block + c]
        return remote(at, at, sib_send.at[block], sib_recv.at[block], sibling)

    def share_in(block):
        at = weight.at[:, 2 * block + 1 - c]
        return remote(at, at, sib_send.at[block], sib_recv.at[block], sibling)

    def send_line(step):
        if step < depth - 1:

            @pl.when((z - step >= 0) & (z + 1 < depth))
            def _():
                line(True, step).start()

            @pl.when((z + step < depth) & (z - 1 >= 0))
            def _():
                line(False, step).start()

    def receive_line(step):
        @pl.when(z - step >= 0)
        def _():
            line_in(True, step).wait_recv()

        @pl.when(z + step < depth)
        def _():
            line_in(False, step).wait_recv()

        send_line(step)

        @pl.when(z - step >= 0)
        def _():
            share(z - step).start()

        @pl.when(z + step < depth)
        def _():
            share(z + step).start()

    def send_part(k):
        return remote(
            part_out.at[k], part_in.at[k], part_send.at[k], part_recv.at[k], sibling
        )

    def send_pair(k, j):
        return remote(
            pair_out.at[k, j],
            pair_in.at[k, j],
            pair_send.at[k, j],
            pair_recv.at[k, j],
            (mate, x, c, y),
        )

    def send_far(k, j):
        return remote(
            far_out.at[k, j],
            far_in.at[k],
            far_send.at[k, j],
            far_recv.at[k],
            (remote_levels[j], x, c, y),
        )

    def send_grad(i, level):
        return remote(
            grads_out.at[1 + i, level],
            grads.at[x, y, level],
            grad_send.at[i, level],
            grad_recv.at[i, level],
            plane[i],
        )

    def grad_in(i, level):
        a, b = owners[i]
        return remote(
            grads_out.at[1 + i, level],
            grads.at[a, b, level],
            grad_send.at[i, level],
            grad_recv.at[i, level],
            plane[i],
        )

    def keep_grad(level):
        return pltpu.make_async_copy(
            grads_out.at[0, level], grads.at[x, y, level], grad_own.at[level]
        )

    take_codes = pltpu.make_async_copy(codes_hbm.at[own_rows()], codes, codes_sem)
    take_scales = pltpu.make_async_copy(scales_hbm, scales_in, scales_sem)
    take_codes.start()
    take_scales.start()
    for group in range(groups):
        for i in range(3):
            load(i, group).start()
    for k in range(chunks):
        own_outputs(k).start()
    pl.semaphore_wait(barrier, len(partners) + middle)
    for k in range(2):
        for way in range(2):
            direct(k, way).start()

    take_codes.wait()
    take_scales.wait()
    scales_ref[...] = scales_in[...].T
    scales = scales_ref[own_rows(), :]
    blocks = scales.shape[1]
    block = chunks * span // blocks
    for b in range(blocks):
        k, at = divmod(b * block, span)
        spread = codes[:, b * block : (b + 1) * block].astype(jnp.float32)
        weight[k, 2 * z + c, :, at : at + block] = (spread * scales[:, b : b + 1]).astype(
            jnp.bfloat16
        )
    send_line(0)
    share(z).start()

    def forward_group(group, carry):
        level, a = group // 2, group % 2
        for i in range(3):
            load(i, group).wait()
        for head in range(heads):
            cols = slice(head * HD, (head + 1) * HD)
            prob = probs_t(ins[0, group, :, cols], ins[1, group, :, cols])
            prob = prob.astype(jnp.bfloat16)
            probs[group * heads + head] = prob
            made = dot(ins[2, group, :, cols], prob, ((0,), (0,))).astype(jnp.bfloat16)
            for core, rep, low, high, at in pieces[head]:
                outgoing[a, rep, level, core, low:high, :] = made[at : at + high - low]

        @pl.when(a == 1)
        def _():
            for i in (2, 0, 1):
                send_context(i, level).start()
            keep_context(level).start()

        return carry

    lax.fori_loop(0, groups, forward_group, 0)

    def weight_part(k, core):
        left = context[:, core].reshape(depth * slab, -1)
        right = near[k].reshape(-1, span)
        return dot(left, right, ((1,), (0,)))

    def grad_part(k, slot):
        left = weight[k].reshape(-1, span)
        return dot(left, near[k, slot], ((1,), (1,)))

    def grad_chunk(k, first):
        def body(slot, carry):
            part = grad_part(k, slot)
            total[slot] = part if first else total[slot] + part
            return carry

        lax.fori_loop(0, 4, body, 0)

    def start_direct(k):
        for way in range(2):
            direct(k, way).start()

    def take_direct(k):
        for way in range(2):
            direct(k, way).wait_recv()
            relay(k, way).start()

    def take_relayed(k):
        own_outputs(k).wait()
        for way in range(2):
            relay(k, way).wait_recv()

    def start_part(k):
        made = weight_part(k, 1 - c).astype(jnp.bfloat16)
        part_out[k] = made.reshape(depth, slab, span)
        send_part(k).start()
        part[...] = weight_part(k, c).reshape(depth, slab, span)

    def finish_part(k):
        send_part(k).wait_recv()

        def summed(level):
            return part[level] + part_in[k, level].astype(jnp.float32)

        @pl.when(middle == 0)
        def _():
            for j in (1, 0):
                pair_out[k, 1 + j] = summed(remote_levels[j]).astype(jnp.bfloat16)
                send_pair(k, 1 + j).start()

        pair_out[k, 0] = summed(mate).astype(jnp.bfloat16)
        send_pair(k, 0).start()

        @pl.when(middle == 1)
        def _():
            for j in range(2):
                far_sum[k, j] = summed(remote_levels[j])

        own_sum[k] = summed(z)

    def pass_far(k):
        @pl.when(middle == 1)
        def _():
            for j in (1, 0):
                send_pair(k, 1 + j).wait_recv()
                both = far_sum[k, j] + pair_in[k, 1 + j].astype(jnp.float32)
                far_out[k, j] = both.astype(jnp.bfloat16)
                send_far(k, j).start()

    def grad_chunk(k, carry):
        def body(slot, inner):
            total[slot] = total[slot] + grad_part(k, slot)
            return inner

        return lax.fori_loop(0, 4, body, carry)

    def end_grad(slot):
        made = (total[slot] + grad_part(last, slot)).astype(jnp.bfloat16)
        grads_out[slot] = made.reshape(depth, CORES, slab, seq)
        for level in range(depth):
            if slot:
                send_grad(slot - 1, level).start()
            else:
                keep_grad(level).start()

    total[...] = jnp.zeros_like(total)
    last, ready = chunks - 1, 2
    receive_line(1)
    take_direct(0)
    start_direct(2)
    receive_line(2)
    for level in range(depth):
        keep_context(level).wait()
        for i in range(3):
            send_context(i, level).wait_recv()

    def chunk(k, carry):
        take_relayed(k)
        take_direct(k + 1)

        @pl.when(k + 3 < chunks)
        def _():
            start_direct(k + 3)

        start_part(k)

        @pl.when(k > 1)
        def _():
            pass_far(k - 2)

        @pl.when(k == ready - 1)
        def _():
            for step in range(3, depth):
                receive_line(step)

        @pl.when(k == ready)
        def _():
            for level in range(depth):
                share_in(level).wait_recv()

        @pl.when((k >= ready) & (k < 2 * ready))
        def _():
            low = 2 * (k - ready)
            lax.fori_loop(low, low + 2, grad_chunk, 0)

        @pl.when(k >= 2 * ready)
        def _():
            grad_chunk(k, 0)

        finish_part(k)
        return carry

    lax.fori_loop(0, last - 1, chunk, 0)
    take_relayed(last - 1)
    take_direct(last)
    grad_chunk(last - 1, 0)
    end_grad(2)
    end_grad(1)
    start_part(last - 1)
    pass_far(last - 3)
    finish_part(last - 1)
    pass_far(last - 2)
    take_relayed(last)
    end_grad(3)
    end_grad(0)
    start_part(last)
    finish_part(last)
    pass_far(last - 1)

    def backward_group(level, a):
        group = 2 * level + a
        for head in range(heads):
            cols = slice(head * HD, (head + 1) * HD)
            query, keyset = ins[0, group, :, cols], ins[1, group, :, cols]
            grad = [
                grads[a, rep, level, core, low:high, :]
                for core, rep, low, high, _ in pieces[head]
            ]
            grad = grad[0] if len(grad) == 1 else jnp.concatenate(grad, axis=0)
            prob = probs[group * heads + head]
            into = pl.ds(pl.multiple_of(group * width + head * HD, HD), HD)
            dv_ref[:, into] = dot(prob, grad, ((1,), (1,))).astype(jnp.bfloat16)
            dprob = dot(ins[2, group, :, cols], grad, ((1,), (0,)))
            prob = prob.astype(jnp.float32)
            delta = jnp.sum(prob * dprob, axis=0, keepdims=True)
            dscore = (prob * (dprob - delta) * SCALE).astype(jnp.bfloat16)
            dk_ref[:, into] = dot(dscore, query, ((1,), (0,))).astype(jnp.bfloat16)
            dq_ref[:, into] = dot(dscore, keyset, ((0,), (0,))).astype(jnp.bfloat16)

    def backward_near(level, carry):
        keep_grad(level).wait()
        grad_in(1, level).wait_recv()
        backward_group(level, x)
        return carry

    def backward_far(level, carry):
        grad_in(0, level).wait_recv()
        grad_in(2, level).wait_recv()
        backward_group(level, 1 - x)
        return carry

    def finish_sum(k, carry):
        send_pair(k, 0).wait_recv()
        send_far(k, 0).wait_recv()
        columns = pl.ds(pl.multiple_of(k * span, span), span)
        both = pair_in[k, 0].astype(jnp.float32) + far_in[k].astype(jnp.float32)
        dw_ref[:, columns] = own_sum[k] + both
        return carry

    lax.fori_loop(0, depth // 2, backward_near, 0)
    pass_far(last)
    lax.fori_loop(depth // 2, depth, backward_near, 0)
    lax.fori_loop(0, last, finish_sum, 0)
    lax.fori_loop(0, depth - 1, backward_far, 0)
    finish_sum(last, 0)
    backward_far(depth - 1, 0)

    def drain_chunk(k, carry):
        for way in range(2):
            direct(k, way).wait_send()
            relay(k, way).wait_send()
        send_part(k).wait_send()
        send_pair(k, 0).wait_send()

        @pl.when(middle == 0)
        def _():
            for j in range(2):
                send_pair(k, 1 + j).wait_send()

        @pl.when(middle == 1)
        def _():
            for j in range(2):
                send_far(k, j).wait_send()

        return carry

    def drain_level(level, carry):
        for i in range(3):
            send_context(i, level).wait_send()
            send_grad(i, level).wait_send()
        share(level).wait_send()
        return carry

    lax.fori_loop(0, chunks, drain_chunk, 0)
    lax.fori_loop(0, depth, drain_level, 0)
    for step in range(depth - 1):

        @pl.when((z - step >= 0) & (z + 1 < depth))
        def _():
            line(True, step).wait_send()

        @pl.when((z + step < depth) & (z - 1 >= 0))
        def _():
            line(False, step).wait_send()


def write_kernel(count, *refs):
    copies = [
        pltpu.make_async_copy(refs[i], refs[count + i], refs[-1].at[i]) for i in range(count)
    ]
    for copy in copies:
        copy.start()
    for copy in copies:
        copy.wait()


def write_out(arrays):
    count = len(arrays)
    anywhere = pl.BlockSpec(memory_space=pl.ANY)
    return pl.pallas_call(
        functools.partial(write_kernel, count),
        in_specs=[anywhere] * count,
        out_specs=[anywhere] * count,
        out_shape=[jax.ShapeDtypeStruct(a.shape, a.dtype) for a in arrays],
        scratch_shapes=[pltpu.SemaphoreType.DMA((count,))],
        compiler_params=pltpu.CompilerParams(vmem_limit_bytes=1 << 20),
        name="write",
    )(*(pltpu.with_memory_space_constraint(a, pltpu.VMEM) for a in arrays))


def head_pieces(width, slab, reps):
    pieces = []
    for head in range(width // HD):
        at, end, found = head * HD, (head + 1) * HD, []
        while at < end:
            block, low = divmod(at, slab)
            count = min(slab - low, end - at)
            found.append((block // reps, block % reps, low, low + count, at - head * HD))
            at += count
        pieces.append(found)
    return pieces


def fits(extents, depth, images, seq, rows, features, blocks):
    if extents != (2, CORES, 2) or images != 1 or depth != 4:
        return False
    slab, span = rows // (depth * 8), features // CHUNKS
    return (
        rows == depth * 8 * slab
        and slab % 16 == 0
        and (4 * slab) % HD == 0
        and features == CHUNKS * span
        and span % (features // blocks) == 0
        and (features // blocks) % 128 == 0
        and seq % 128 == 0
    )


def fused(queries, keys, values, grad_output, weight_codes, weight_scales):
    _, seq, rows = queries.shape
    features = grad_output.shape[-1]
    depth = lax.axis_size("z")
    slab, span = rows // (depth * 8), features // CHUNKS
    width = 4 * slab
    groups, heads = 2 * depth, width // HD
    half, whole = jnp.bfloat16, jnp.float32
    dma = pltpu.SemaphoreType.DMA
    anywhere = pl.BlockSpec(memory_space=pl.ANY)
    blocks = weight_scales.shape[-1]
    image = pltpu.VMEM((seq, rows), half)
    scratch = [
        pltpu.VMEM((3, groups, seq, width), half),
        pltpu.VMEM((slab, features), half),
        pltpu.VMEM((blocks, 2 * slab), whole),
        pltpu.VMEM((2 * slab, blocks), whole),
        pltpu.VMEM((CHUNKS, 4, seq, span), half),
        pltpu.VMEM((CHUNKS, 2 * depth, slab, span), half),
        pltpu.VMEM((depth, CORES, slab, 4 * seq), half),
        pltpu.VMEM((2, 2, depth, CORES, slab, seq), half),
        pltpu.VMEM((4, rows // 4, seq), whole),
        pltpu.VMEM((4, depth, CORES, slab, seq), half),
        pltpu.VMEM((2, 2, depth, CORES, slab, seq), half),
        pltpu.VMEM((CHUNKS, depth, slab, span), half),
        pltpu.VMEM((CHUNKS, depth, slab, span), half),
        pltpu.VMEM((CHUNKS, 3, slab, span), half),
        pltpu.VMEM((CHUNKS, 3, slab, span), half),
        pltpu.VMEM((CHUNKS, 2, slab, span), whole),
        pltpu.VMEM((CHUNKS, 2, slab, span), half),
        pltpu.VMEM((CHUNKS, slab, span), half),
        pltpu.VMEM((CHUNKS, slab, span), whole),
        pltpu.VMEM((depth, slab, span), whole),
        pltpu.VMEM((groups * heads, seq, seq), half),
        dma((3, groups)),
        dma,
        dma,
        dma((CHUNKS,)),
        dma((2, CHUNKS)),
        dma((2, CHUNKS)),
        dma((2, CHUNKS)),
        dma((2, CHUNKS)),
        dma((3, depth)),
        dma((3, depth)),
        dma((depth,)),
        dma((2, depth - 1)),
        dma((2, depth - 1)),
        dma((depth,)),
        dma((depth,)),
        dma((CHUNKS,)),
        dma((CHUNKS,)),
        dma((CHUNKS, 3)),
        dma((CHUNKS, 3)),
        dma((CHUNKS, 2)),
        dma((CHUNKS,)),
        dma((3, depth)),
        dma((3, depth)),
        dma((depth,)),
    ]
    made = pl.pallas_call(
        functools.partial(fused_kernel, depth, CHUNKS, head_pieces(width, slab, 2)),
        in_specs=[anywhere] * 6,
        out_specs=[pl.BlockSpec(memory_space=pltpu.VMEM)] * 4,
        out_shape=[image] * 3 + [pltpu.VMEM((slab, features), whole)],
        scratch_shapes=scratch,
        compiler_params=pltpu.CompilerParams(
            collective_id=0, has_side_effects=True, vmem_limit_bytes=48 << 20
        ),
        name="fused",
    )(queries[0], keys[0], values[0], grad_output[0], weight_codes, weight_scales.T)
    *grads, total = write_out(made)
    return (*(grad[None] for grad in grads), total)


def per_device(queries, keys, values, grad_output, weight_codes, weight_scales):
    image_count, seq, rows = queries.shape
    depth = lax.axis_size("z")
    extents = tuple(lax.axis_size(axis) for axis in PLANE)
    sizes = (image_count, seq, rows, grad_output.shape[-1], weight_scales.shape[-1])
    if fits(extents, depth, *sizes):
        return fused(queries, keys, values, grad_output, weight_codes, weight_scales)
    home = tuple(lax.axis_index(axis) for axis in PLANE)
    replicas, peers = extents[-1], math.prod(extents)
    slab = rows // (depth * peers)
    share = depth * slab
    steps = list(itertools.product(*(range(n) for n in extents)))

    def shifted(value, step):
        pairs = []
        for source, place in enumerate(steps):
            to = 0
            for at, move, n in zip(place, step, extents):
                to = to * n + (at + move) % n
            pairs.append((source, to))
        return lax.ppermute(value, PLANE, pairs)

    def start_at(step):
        return (0, *((h + s) % n for h, s, n in zip(home, step, extents)), 0, 0)

    own = home[-1] * slab
    codes = lax.dynamic_slice_in_dim(weight_codes, own, slab, 0)
    scales = lax.dynamic_slice_in_dim(weight_scales, own, slab, 0)
    weight = lax.all_gather(restore(codes, scales), "z", axis=0, tiled=True)

    kept = []
    for image in range(image_count):
        first = grad_output[image]
        straight = [shifted(first, (0, 0, r)) for r in range(1, replicas)]
        across = shifted(first, (1, 0, 0))
        context = forward(queries[image], keys[image], values[image])
        context = context.reshape(depth, *extents, slab, seq)
        pieces = [
            lax.dynamic_slice(context, start_at(step), (depth, 1, 1, 1, slab, seq)).reshape(
                share, seq
            )
            for step in steps
        ]
        contexts = [pieces[0]] + [shifted(p, step) for p, step in zip(pieces[1:], steps[1:])]
        across, straight, _ = lax.optimization_barrier((across, straight, pieces[0]))
        half = seq // 2
        corner = [
            jnp.concatenate(
                [shifted(piece[:half], (1, 0, 0)), shifted(across[half:], (0, 0, r))]
            )
            for r, piece in enumerate(straight, 1)
        ]
        near = {(0, 0): first, (1, 0): across}
        for r in range(1, replicas):
            near[0, r], near[1, r] = straight[r - 1], corner[r - 1]
        outputs = [
            near[x, r] if c == 0 else shifted(near[x, r], (0, 1, 0)) for x, c, r in steps
        ]
        kept.append((outputs, contexts))
    terms = weight_terms(
        [c for pair in kept for c in pair[1]], [o for pair in kept for o in pair[0]]
    )
    total = lax.psum_scatter(terms, "z", scatter_dimension=0, tiled=True)
    results = []
    for image in range(image_count):
        grad = jnp.zeros((depth, *extents, slab, seq), jnp.bfloat16)
        for step, output in zip(steps, kept[image][0]):
            piece = dot(weight, output, ((1,), (1,))).astype(jnp.bfloat16)
            if any(step):
                piece = shifted(piece, tuple(-s for s in step))
            grad = lax.dynamic_update_slice(
                grad, piece.reshape(depth, 1, 1, 1, slab, seq), start_at(step)
            )
        results.append(
            backward(queries[image], keys[image], values[image], grad.reshape(rows, seq))
        )
    grads = [
        parts[0][None] if image_count == 1 else jnp.stack(parts) for parts in zip(*results)
    ]
    return (*grads, total.astype(jnp.float32))


def solution(mesh):
    groups, replicas = mesh.shape["group"], mesh.shape["rep"]
    split = Mesh(
        mesh.devices.reshape(groups // (2 * CORES), 2, CORES, replicas), ("z", *PLANE)
    )
    images = P(("z", *PLANE), None, None)
    shards = P(("z", "x", "core"), None)
    return jax.shard_map(
        per_device,
        mesh=split,
        in_specs=(images,) * 4 + (shards,) * 2,
        out_specs=(images,) * 3 + (P(("z", *PLANE), None),),
        check_vma=False,
    )
```

```python
import functools
import itertools
import math

import jax
import jax.numpy as jnp
from jax import lax
from jax.experimental import pallas as pl
from jax.experimental.pallas import tpu as pltpu
from jax.sharding import Mesh, PartitionSpec as P

HD = 128
SCALE = HD ** (-0.5)
CORES = 2
PLANE = ("x", "core", "rep")


def dot(a, b, dims):
    return lax.dot_general(a, b, (dims, ((), ())), preferred_element_type=jnp.float32)


def probs_t(query, keyset):
    scores = dot(keyset, query, ((1,), (1,)))
    highest = jnp.max(scores, axis=0, keepdims=True)
    exponent = jnp.exp2((scores - highest) * (SCALE * math.log2(math.e)))
    return exponent * (1.0 / jnp.sum(exponent, axis=0, keepdims=True))


def forward_kernel(heads, q_ref, k_ref, v_ref, ctx_ref):
    for head in range(heads):
        cols = slice(head * HD, (head + 1) * HD)
        prob = probs_t(q_ref[:, cols], k_ref[:, cols]).astype(jnp.bfloat16)
        ctx_ref[cols, :] = dot(v_ref[:, cols], prob, ((0,), (0,))).astype(jnp.bfloat16)


def backward_kernel(heads, q_ref, k_ref, v_ref, g_ref, dq_ref, dk_ref, dv_ref):
    for head in range(heads):
        cols = slice(head * HD, (head + 1) * HD)
        query, keyset, grad = q_ref[:, cols], k_ref[:, cols], g_ref[cols, :]
        prob = probs_t(query, keyset)
        dv_ref[:, cols] = dot(prob.astype(jnp.bfloat16), grad, ((1,), (1,))).astype(jnp.bfloat16)
        dprob = dot(v_ref[:, cols], grad, ((1,), (0,)))
        delta = jnp.sum(prob * dprob, axis=0, keepdims=True)
        dscore = (prob * (dprob - delta) * SCALE).astype(jnp.bfloat16)
        dk_ref[:, cols] = dot(dscore, query, ((1,), (0,))).astype(jnp.bfloat16)
        dq_ref[:, cols] = dot(dscore, keyset, ((0,), (0,))).astype(jnp.bfloat16)


def heads_per_step(head_count):
    return next(n for n in (4, 3, 2, 1) if head_count % n == 0)


def forward(query, keyset, valueset):
    seq, rows = query.shape
    heads = heads_per_step(rows // HD)
    wide = pl.BlockSpec((seq, heads * HD), lambda i: (0, i))
    return pl.pallas_call(
        functools.partial(forward_kernel, heads),
        grid=(rows // (heads * HD),),
        in_specs=[wide] * 3,
        out_specs=pl.BlockSpec((heads * HD, seq), lambda i: (i, 0)),
        out_shape=jax.ShapeDtypeStruct((rows, seq), jnp.bfloat16),
        cost_estimate=pl.CostEstimate(
            flops=4 * seq * seq * rows,
            bytes_accessed=8 * seq * rows,
            transcendentals=seq * seq * rows // HD,
        ),
        name="forward",
    )(query, keyset, valueset)


def backward(query, keyset, valueset, grad_t):
    seq, rows = query.shape
    heads = heads_per_step(rows // HD)
    wide = pl.BlockSpec((seq, heads * HD), lambda i: (0, i))
    return pl.pallas_call(
        functools.partial(backward_kernel, heads),
        grid=(rows // (heads * HD),),
        in_specs=[wide] * 3 + [pl.BlockSpec((heads * HD, seq), lambda i: (i, 0))],
        out_specs=[wide] * 3,
        out_shape=[jax.ShapeDtypeStruct((seq, rows), jnp.bfloat16)] * 3,
        cost_estimate=pl.CostEstimate(
            flops=10 * seq * seq * rows,
            bytes_accessed=14 * seq * rows,
            transcendentals=seq * seq * rows // HD,
        ),
        name="backward",
    )(query, keyset, valueset, grad_t)


def term_kernel(count, *refs):
    total = None
    for i in range(count):
        part = dot(refs[i][...], refs[count + i][...], ((1,), (0,)))
        total = part if total is None else total + part
    refs[-1][...] = total.astype(jnp.bfloat16)


def weight_terms(contexts, outputs):
    count = len(contexts)
    rows, seq = contexts[0].shape
    features = outputs[0].shape[1]
    tile = math.gcd(features, 512)
    return pl.pallas_call(
        functools.partial(term_kernel, count),
        grid=(features // tile,),
        in_specs=[pl.BlockSpec((rows, seq), lambda i: (0, 0))] * count
        + [pl.BlockSpec((seq, tile), lambda i: (0, i))] * count,
        out_specs=pl.BlockSpec((rows, tile), lambda i: (0, i)),
        out_shape=jax.ShapeDtypeStruct((rows, features), jnp.bfloat16),
        cost_estimate=pl.CostEstimate(
            flops=2 * rows * seq * features * count,
            bytes_accessed=2 * (count * seq * (rows + features) + rows * features),
            transcendentals=0,
        ),
        name="terms",
    )(*contexts, *outputs)


def restore(codes, scales):
    rows, blocks = scales.shape
    spread = codes.astype(jnp.float32).reshape(rows, blocks, -1) * scales[:, :, None]
    return spread.reshape(rows, -1).astype(jnp.bfloat16)


MESH_ID = pl.DeviceIdType.MESH
AXES = ("z", "x", "core", "rep")
CHUNKS = 6


def fused_kernel(
    depth,
    chunks,
    pieces,
    q_hbm,
    k_hbm,
    v_hbm,
    g_hbm,
    codes_hbm,
    scales_hbm,
    dq_ref,
    dk_ref,
    dv_ref,
    dw_ref,
    tail_ins,
    tail_grads,
    tail_probs,
    ins,
    codes,
    scales_in,
    scales_ref,
    near,
    weight,
    context,
    outgoing,
    total,
    grads_out,
    grads,
    part_out,
    part_in,
    pair_out,
    pair_in,
    far_sum,
    far_out,
    far_in,
    own_sum,
    part,
    probs,
    in_sem,
    codes_sem,
    scales_sem,
    own_sem,
    direct_send,
    direct_recv,
    relay_send,
    relay_recv,
    ctx_send,
    ctx_recv,
    ctx_own,
    line_send,
    line_recv,
    sib_send,
    sib_recv,
    part_send,
    part_recv,
    pair_send,
    pair_recv,
    far_send,
    far_recv,
    grad_send,
    grad_recv,
    grad_own,
):
    z, x, c, y = (lax.axis_index(axis) for axis in AXES)
    groups, seq, width = ins.shape[1:]
    heads = width // HD
    slab = codes.shape[0]
    span = near.shape[-1]
    half = seq // 2
    across, along, corner = (z, 1 - x, c, y), (z, x, c, 1 - y), (z, 1 - x, c, 1 - y)
    sibling = (z, x, 1 - c, y)
    plane = (across, along, corner)
    owners = ((1 - x, y), (x, 1 - y), (1 - x, 1 - y))
    mate, far = z + 1 - 2 * (z % 2), (z + 2) % depth
    middle = (z % 2 - z // 2) * (z % 2 - z // 2)
    remote_levels = (2 - z // 2, (depth - 1) * (1 - z // 2))

    barrier = pltpu.get_barrier_semaphore()
    partners = [*plane, sibling, (mate, x, c, y), (far, x, c, y)]
    for partner in partners:
        pl.semaphore_signal(barrier, inc=1, device_id=partner, device_id_type=MESH_ID)

    @pl.when(middle == 1)
    def _():
        other = (depth - 1 - z, x, c, y)
        pl.semaphore_signal(barrier, inc=1, device_id=other, device_id_type=MESH_ID)

    def remote(source, target, send, recv, device):
        return pltpu.make_async_remote_copy(
            src_ref=source,
            dst_ref=target,
            send_sem=send,
            recv_sem=recv,
            device_id=device,
            device_id_type=MESH_ID,
        )

    def own_rows():
        return pl.ds(pl.multiple_of(y * slab, slab), slab)

    def load(i, group):
        source = (q_hbm, k_hbm, v_hbm)[i]
        columns = pl.ds(pl.multiple_of(group * width, width), width)
        return pltpu.make_async_copy(
            source.at[:, columns], ins.at[i, group], in_sem.at[i, group]
        )

    def own_outputs(k):
        columns = pl.ds(pl.multiple_of(k * span, span), span)
        return pltpu.make_async_copy(g_hbm.at[:, columns], near.at[k, 0], own_sem.at[k])

    def direct(k, way):
        columns = pl.ds(pl.multiple_of(k * span, span), span)
        return remote(
            g_hbm.at[:, columns],
            near.at[k, 1 + way],
            direct_send.at[way, k],
            direct_recv.at[way, k],
            plane[way],
        )

    def relay(k, way):
        rows = pl.ds(way * half, half)
        return remote(
            near.at[k, 1 + way, rows],
            near.at[k, 3, rows],
            relay_send.at[way, k],
            relay_recv.at[way, k],
            plane[1 - way],
        )

    def send_context(i, level):
        a, b = owners[i]
        return remote(
            outgoing.at[a, b, level],
            context.at[level, :, :, pl.ds((1 + i) * seq, seq)],
            ctx_send.at[i, level],
            ctx_recv.at[i, level],
            plane[i],
        )

    def keep_context(level):
        return pltpu.make_async_copy(
            outgoing.at[x, y, level],
            context.at[level, :, :, pl.ds(0, seq)],
            ctx_own.at[level],
        )

    def line(up, step):
        block = z - step if up else z + step
        at = weight.at[:, 2 * block + c]
        way = 0 if up else 1
        target = (z + 1 if up else z - 1, x, c, y)
        return remote(at, at, line_send.at[way, step], line_recv.at[way, step], target)

    def line_in(up, step):
        block = z - step if up else z + step
        at = weight.at[:, 2 * block + c]
        way = 0 if up else 1
        target = (z + 1 if up else z - 1, x, c, y)
        return remote(
            at, at, line_send.at[way, step - 1], line_recv.at[way, step - 1], target
        )

    def share(block):
        at = weight.at[:, 2 * block + c]
        return remote(at, at, sib_send.at[block], sib_recv.at[block], sibling)

    def share_in(block):
        at = weight.at[:, 2 * block + 1 - c]
        return remote(at, at, sib_send.at[block], sib_recv.at[block], sibling)

    def send_line(step):
        if step < depth - 1:

            @pl.when((z - step >= 0) & (z + 1 < depth))
            def _():
                line(True, step).start()

            @pl.when((z + step < depth) & (z - 1 >= 0))
            def _():
                line(False, step).start()

    def receive_line(step):
        @pl.when(z - step >= 0)
        def _():
            line_in(True, step).wait_recv()

        @pl.when(z + step < depth)
        def _():
            line_in(False, step).wait_recv()

        send_line(step)

        @pl.when(z - step >= 0)
        def _():
            share(z - step).start()

        @pl.when(z + step < depth)
        def _():
            share(z + step).start()

    def send_part(k):
        return remote(
            part_out.at[k], part_in.at[k], part_send.at[k], part_recv.at[k], sibling
        )

    def send_pair(k, j):
        return remote(
            pair_out.at[k, j],
            pair_in.at[k, j],
            pair_send.at[k, j],
            pair_recv.at[k, j],
            (mate, x, c, y),
        )

    def send_far(k, j):
        return remote(
            far_out.at[k, j],
            far_in.at[k],
            far_send.at[k, j],
            far_recv.at[k],
            (remote_levels[j], x, c, y),
        )

    def send_grad(i, level):
        return remote(
            grads_out.at[1 + i, level],
            grads.at[x, y, level],
            grad_send.at[i, level],
            grad_recv.at[i, level],
            plane[i],
        )

    def grad_in(i, level):
        a, b = owners[i]
        return remote(
            grads_out.at[1 + i, level],
            grads.at[a, b, level],
            grad_send.at[i, level],
            grad_recv.at[i, level],
            plane[i],
        )

    def keep_grad(level):
        return pltpu.make_async_copy(
            grads_out.at[0, level], grads.at[x, y, level], grad_own.at[level]
        )

    take_codes = pltpu.make_async_copy(codes_hbm.at[own_rows()], codes, codes_sem)
    take_scales = pltpu.make_async_copy(scales_hbm, scales_in, scales_sem)
    take_codes.start()
    take_scales.start()
    for group in range(groups):
        for i in range(3):
            load(i, group).start()
    for k in range(chunks):
        own_outputs(k).start()
    pl.semaphore_wait(barrier, len(partners) + middle)
    for k in range(2):
        for way in range(2):
            direct(k, way).start()

    take_codes.wait()
    take_scales.wait()
    scales_ref[...] = scales_in[...].T
    scales = scales_ref[own_rows(), :]
    blocks = scales.shape[1]
    block = chunks * span // blocks
    for b in range(blocks):
        k, at = divmod(b * block, span)
        spread = codes[:, b * block : (b + 1) * block].astype(jnp.float32)
        weight[k, 2 * z + c, :, at : at + block] = (spread * scales[:, b : b + 1]).astype(
            jnp.bfloat16
        )
    send_line(0)
    share(z).start()

    def forward_group(group, carry):
        level, a = group // 2, group % 2
        for i in range(3):
            load(i, group).wait()
        for head in range(heads):
            cols = slice(head * HD, (head + 1) * HD)
            prob = probs_t(ins[0, group, :, cols], ins[1, group, :, cols])
            prob = prob.astype(jnp.bfloat16)
            probs[group * heads + head] = prob
            made = dot(ins[2, group, :, cols], prob, ((0,), (0,))).astype(jnp.bfloat16)
            for core, rep, low, high, at in pieces[head]:
                outgoing[a, rep, level, core, low:high, :] = made[at : at + high - low]

        @pl.when(a == 1)
        def _():
            for i in (2, 0, 1):
                send_context(i, level).start()
            keep_context(level).start()

        return carry

    lax.fori_loop(0, groups, forward_group, 0)

    def weight_part(k, core):
        left = context[:, core].reshape(depth * slab, -1)
        right = near[k].reshape(-1, span)
        return dot(left, right, ((1,), (0,)))

    def grad_part(k, slot):
        left = weight[k].reshape(-1, span)
        return dot(left, near[k, slot], ((1,), (1,)))

    def grad_chunk(k, first):
        def body(slot, carry):
            part = grad_part(k, slot)
            total[slot] = part if first else total[slot] + part
            return carry

        lax.fori_loop(0, 4, body, 0)

    def start_direct(k):
        for way in range(2):
            direct(k, way).start()

    def take_direct(k):
        for way in range(2):
            direct(k, way).wait_recv()
            relay(k, way).start()

    def take_relayed(k):
        own_outputs(k).wait()
        for way in range(2):
            relay(k, way).wait_recv()

    def start_part(k):
        made = weight_part(k, 1 - c).astype(jnp.bfloat16)
        part_out[k] = made.reshape(depth, slab, span)
        send_part(k).start()
        part[...] = weight_part(k, c).reshape(depth, slab, span)

    def finish_part(k):
        send_part(k).wait_recv()

        def summed(level):
            return part[level] + part_in[k, level].astype(jnp.float32)

        @pl.when(middle == 0)
        def _():
            for j in (1, 0):
                pair_out[k, 1 + j] = summed(remote_levels[j]).astype(jnp.bfloat16)
                send_pair(k, 1 + j).start()

        pair_out[k, 0] = summed(mate).astype(jnp.bfloat16)
        send_pair(k, 0).start()

        @pl.when(middle == 1)
        def _():
            for j in range(2):
                far_sum[k, j] = summed(remote_levels[j])

        own_sum[k] = summed(z)

    def pass_far(k):
        @pl.when(middle == 1)
        def _():
            for j in (1, 0):
                send_pair(k, 1 + j).wait_recv()
                both = far_sum[k, j] + pair_in[k, 1 + j].astype(jnp.float32)
                far_out[k, j] = both.astype(jnp.bfloat16)
                send_far(k, j).start()

    def grad_chunk(k, carry):
        def body(slot, inner):
            total[slot] = total[slot] + grad_part(k, slot)
            return inner

        return lax.fori_loop(0, 4, body, carry)

    def end_grad(slot):
        made = total[slot]
        for k in range(last if slot == 3 else last - 1, chunks):
            made = made + grad_part(k, slot)
        made = made.astype(jnp.bfloat16)
        grads_out[slot] = made.reshape(depth, CORES, slab, seq)
        for level in range(depth):
            if slot:
                send_grad(slot - 1, level).start()
            else:
                keep_grad(level).start()

    total[...] = jnp.zeros_like(total)
    last, ready = chunks - 1, 2
    receive_line(1)
    take_direct(0)
    start_direct(2)
    receive_line(2)
    for level in range(depth):
        keep_context(level).wait()
        for i in range(3):
            send_context(i, level).wait_recv()

    def chunk(k, carry):
        take_direct(k + 1)

        @pl.when(k + 3 < chunks)
        def _():
            start_direct(k + 3)

        take_relayed(k)
        start_part(k)

        @pl.when(k > 1)
        def _():
            pass_far(k - 2)

        @pl.when(k == ready - 1)
        def _():
            for step in range(3, depth):
                receive_line(step)

        @pl.when(k == ready)
        def _():
            for level in range(depth):
                share_in(level).wait_recv()

        @pl.when((k >= ready) & (k < 2 * ready))
        def _():
            low = 2 * (k - ready)
            lax.fori_loop(low, low + 2, grad_chunk, 0)

        @pl.when(k >= 2 * ready)
        def _():
            grad_chunk(k, 0)

        finish_part(k)
        return carry

    lax.fori_loop(0, last - 1, chunk, 0)
    take_direct(last)
    end_grad(2)
    end_grad(1)
    take_relayed(last - 1)
    start_part(last - 1)
    total[3] = total[3] + grad_part(last - 1, 3)
    pass_far(last - 3)
    finish_part(last - 1)
    pass_far(last - 2)
    take_relayed(last)
    end_grad(3)
    start_part(last)
    end_grad(0)
    finish_part(last)
    pass_far(last - 1)

    def backward_group(level, a):
        group = 2 * level + a
        for head in range(heads):
            into = pl.ds(pl.multiple_of(group * width + head * HD, HD), HD)
            dq_ref[:, into], dk_ref[:, into], dv_ref[:, into] = backward_head(
                ins.at[:, group],
                grads.at[a, :, level],
                probs.at[group * heads + head],
                pieces[head],
                head,
            )

    def backward_near(level, carry):
        keep_grad(level).wait()
        grad_in(1, level).wait_recv()
        backward_group(level, x)
        return carry

    def backward_far(level, carry):
        grad_in(0, level).wait_recv()
        grad_in(2, level).wait_recv()
        backward_group(level, 1 - x)
        return carry

    def finish_sum(k, carry):
        send_pair(k, 0).wait_recv()
        send_far(k, 0).wait_recv()
        columns = pl.ds(pl.multiple_of(k * span, span), span)
        both = pair_in[k, 0].astype(jnp.float32) + far_in[k].astype(jnp.float32)
        dw_ref[:, columns] = own_sum[k] + both
        return carry

    lax.fori_loop(0, depth // 2, backward_near, 0)
    pass_far(last)
    lax.fori_loop(depth // 2, depth, backward_near, 0)
    lax.fori_loop(0, last, finish_sum, 0)
    lax.fori_loop(0, depth - 1, backward_far, 0)
    finish_sum(last, 0)
    group = 2 * (depth - 1) + 1 - x
    tail_ins[...] = ins[:, group]
    tail_probs[...] = probs[pl.ds(group * heads, heads)]
    grad_in(0, depth - 1).wait_recv()
    grad_in(2, depth - 1).wait_recv()
    tail_grads[...] = grads[1 - x, :, depth - 1]

    def drain_chunk(k, carry):
        for way in range(2):
            direct(k, way).wait_send()
            relay(k, way).wait_send()
        send_part(k).wait_send()
        send_pair(k, 0).wait_send()

        @pl.when(middle == 0)
        def _():
            for j in range(2):
                send_pair(k, 1 + j).wait_send()

        @pl.when(middle == 1)
        def _():
            for j in range(2):
                send_far(k, j).wait_send()

        return carry

    def drain_level(level, carry):
        for i in range(3):
            send_context(i, level).wait_send()
            send_grad(i, level).wait_send()
        share(level).wait_send()
        return carry

    lax.fori_loop(0, chunks, drain_chunk, 0)
    lax.fori_loop(0, depth, drain_level, 0)
    for step in range(depth - 1):

        @pl.when((z - step >= 0) & (z + 1 < depth))
        def _():
            line(True, step).wait_send()

        @pl.when((z + step < depth) & (z - 1 >= 0))
        def _():
            line(False, step).wait_send()


def backward_head(ins_ref, grads_ref, probs_ref, pieces, head):
    cols = slice(head * HD, (head + 1) * HD)
    query, keyset = ins_ref[0, :, cols], ins_ref[1, :, cols]
    grad = [grads_ref[rep, core, low:high, :] for core, rep, low, high, _ in pieces]
    grad = grad[0] if len(grad) == 1 else jnp.concatenate(grad, axis=0)
    prob = probs_ref[...]
    dv = dot(prob, grad, ((1,), (1,))).astype(jnp.bfloat16)
    dprob = dot(ins_ref[2, :, cols], grad, ((1,), (0,)))
    prob = prob.astype(jnp.float32)
    delta = jnp.sum(prob * dprob, axis=0, keepdims=True)
    dscore = (prob * (dprob - delta) * SCALE).astype(jnp.bfloat16)
    dk = dot(dscore, query, ((1,), (0,))).astype(jnp.bfloat16)
    dq = dot(dscore, keyset, ((0,), (0,))).astype(jnp.bfloat16)
    return dq, dk, dv


def tail_kernel(depth, pieces, *refs):
    made, total, (ins, grads, probs), outs, dw = refs[:3], refs[3], refs[4:7], refs[7:10], refs[10]
    last, sem = refs[11:]
    width = ins.shape[-1]
    x = lax.axis_index("x")
    most = 2 * (depth - 1) * width
    near = pl.ds(pl.multiple_of(most + x * width, width), width)
    far = pl.ds(pl.multiple_of(most + (1 - x) * width, width), width)
    copies = [pltpu.make_async_copy(total, dw, sem.at[3, 0])]
    for i in range(3):
        for j, at in enumerate((pl.ds(0, most), near)):
            copies.append(
                pltpu.make_async_copy(made[i].at[:, at], outs[i].at[:, at], sem.at[i, j])
            )
    for copy in copies:
        copy.start()
    for head in range(len(pieces)):
        cols = slice(head * HD, (head + 1) * HD)
        last[0, :, cols], last[1, :, cols], last[2, :, cols] = backward_head(
            ins, grads, probs.at[head], pieces[head], head
        )
    for i in range(3):
        copy = pltpu.make_async_copy(last.at[i], outs[i].at[:, far], sem.at[i, 2])
        copy.start()
        copies.append(copy)
    for copy in copies:
        copy.wait()


def write_out(depth, pieces, arrays):
    anywhere = pl.BlockSpec(memory_space=pl.ANY)
    within = pl.BlockSpec(memory_space=pltpu.VMEM)
    return pl.pallas_call(
        functools.partial(tail_kernel, depth, pieces),
        in_specs=[anywhere] * 4 + [within] * 3,
        out_specs=[anywhere] * 4,
        out_shape=[jax.ShapeDtypeStruct(a.shape, a.dtype) for a in arrays[:4]],
        scratch_shapes=[
            pltpu.VMEM(arrays[4].shape, arrays[4].dtype),
            pltpu.SemaphoreType.DMA((4, 3)),
        ],
        compiler_params=pltpu.CompilerParams(vmem_limit_bytes=4 << 20),
        name="tail",
    )(*(pltpu.with_memory_space_constraint(a, pltpu.VMEM) for a in arrays))


def head_pieces(width, slab, reps):
    pieces = []
    for head in range(width // HD):
        at, end, found = head * HD, (head + 1) * HD, []
        while at < end:
            block, low = divmod(at, slab)
            count = min(slab - low, end - at)
            found.append((block // reps, block % reps, low, low + count, at - head * HD))
            at += count
        pieces.append(found)
    return pieces


def fits(extents, depth, images, seq, rows, features, blocks):
    if extents != (2, CORES, 2) or images != 1 or depth != 4:
        return False
    slab, span = rows // (depth * 8), features // CHUNKS
    return (
        rows == depth * 8 * slab
        and slab % 16 == 0
        and (4 * slab) % HD == 0
        and features == CHUNKS * span
        and span % (features // blocks) == 0
        and (features // blocks) % 128 == 0
        and seq % 128 == 0
    )


def fused(queries, keys, values, grad_output, weight_codes, weight_scales):
    _, seq, rows = queries.shape
    features = grad_output.shape[-1]
    depth = lax.axis_size("z")
    slab, span = rows // (depth * 8), features // CHUNKS
    width = 4 * slab
    groups, heads = 2 * depth, width // HD
    half, whole = jnp.bfloat16, jnp.float32
    dma = pltpu.SemaphoreType.DMA
    anywhere = pl.BlockSpec(memory_space=pl.ANY)
    blocks = weight_scales.shape[-1]
    image = pltpu.VMEM((seq, rows), half)
    pieces = head_pieces(width, slab, 2)
    scratch = [
        pltpu.VMEM((3, groups, seq, width), half),
        pltpu.VMEM((slab, features), half),
        pltpu.VMEM((blocks, 2 * slab), whole),
        pltpu.VMEM((2 * slab, blocks), whole),
        pltpu.VMEM((CHUNKS, 4, seq, span), half),
        pltpu.VMEM((CHUNKS, 2 * depth, slab, span), half),
        pltpu.VMEM((depth, CORES, slab, 4 * seq), half),
        pltpu.VMEM((2, 2, depth, CORES, slab, seq), half),
        pltpu.VMEM((4, rows // 4, seq), whole),
        pltpu.VMEM((4, depth, CORES, slab, seq), half),
        pltpu.VMEM((2, 2, depth, CORES, slab, seq), half),
        pltpu.VMEM((CHUNKS, depth, slab, span), half),
        pltpu.VMEM((CHUNKS, depth, slab, span), half),
        pltpu.VMEM((CHUNKS, 3, slab, span), half),
        pltpu.VMEM((CHUNKS, 3, slab, span), half),
        pltpu.VMEM((CHUNKS, 2, slab, span), whole),
        pltpu.VMEM((CHUNKS, 2, slab, span), half),
        pltpu.VMEM((CHUNKS, slab, span), half),
        pltpu.VMEM((CHUNKS, slab, span), whole),
        pltpu.VMEM((depth, slab, span), whole),
        pltpu.VMEM((groups * heads, seq, seq), half),
        dma((3, groups)),
        dma,
        dma,
        dma((CHUNKS,)),
        dma((2, CHUNKS)),
        dma((2, CHUNKS)),
        dma((2, CHUNKS)),
        dma((2, CHUNKS)),
        dma((3, depth)),
        dma((3, depth)),
        dma((depth,)),
        dma((2, depth - 1)),
        dma((2, depth - 1)),
        dma((depth,)),
        dma((depth,)),
        dma((CHUNKS,)),
        dma((CHUNKS,)),
        dma((CHUNKS, 3)),
        dma((CHUNKS, 3)),
        dma((CHUNKS, 2)),
        dma((CHUNKS,)),
        dma((3, depth)),
        dma((3, depth)),
        dma((depth,)),
    ]
    made = pl.pallas_call(
        functools.partial(fused_kernel, depth, CHUNKS, pieces),
        in_specs=[anywhere] * 6,
        out_specs=[pl.BlockSpec(memory_space=pltpu.VMEM)] * 7,
        out_shape=[image] * 3
        + [
            pltpu.VMEM((slab, features), whole),
            pltpu.VMEM((3, seq, width), half),
            pltpu.VMEM((2, CORES, slab, seq), half),
            pltpu.VMEM((heads, seq, seq), half),
        ],
        scratch_shapes=scratch,
        compiler_params=pltpu.CompilerParams(
            collective_id=0, has_side_effects=True, vmem_limit_bytes=48 << 20
        ),
        name="fused",
    )(
        queries[0],
        keys[0],
        values[0],
        grad_output[0],
        weight_codes,
        pltpu.with_memory_space_constraint(weight_scales.T, pltpu.HBM),
    )
    *grads, total = write_out(depth, pieces, made)
    return (*(grad[None] for grad in grads), total)


def per_device(queries, keys, values, grad_output, weight_codes, weight_scales):
    image_count, seq, rows = queries.shape
    depth = lax.axis_size("z")
    extents = tuple(lax.axis_size(axis) for axis in PLANE)
    sizes = (image_count, seq, rows, grad_output.shape[-1], weight_scales.shape[-1])
    if fits(extents, depth, *sizes):
        return fused(queries, keys, values, grad_output, weight_codes, weight_scales)
    home = tuple(lax.axis_index(axis) for axis in PLANE)
    replicas, peers = extents[-1], math.prod(extents)
    slab = rows // (depth * peers)
    share = depth * slab
    steps = list(itertools.product(*(range(n) for n in extents)))

    def shifted(value, step):
        pairs = []
        for source, place in enumerate(steps):
            to = 0
            for at, move, n in zip(place, step, extents):
                to = to * n + (at + move) % n
            pairs.append((source, to))
        return lax.ppermute(value, PLANE, pairs)

    def start_at(step):
        return (0, *((h + s) % n for h, s, n in zip(home, step, extents)), 0, 0)

    own = home[-1] * slab
    codes = lax.dynamic_slice_in_dim(weight_codes, own, slab, 0)
    scales = lax.dynamic_slice_in_dim(weight_scales, own, slab, 0)
    weight = lax.all_gather(restore(codes, scales), "z", axis=0, tiled=True)

    kept = []
    for image in range(image_count):
        first = grad_output[image]
        straight = [shifted(first, (0, 0, r)) for r in range(1, replicas)]
        across = shifted(first, (1, 0, 0))
        context = forward(queries[image], keys[image], values[image])
        context = context.reshape(depth, *extents, slab, seq)
        pieces = [
            lax.dynamic_slice(context, start_at(step), (depth, 1, 1, 1, slab, seq)).reshape(
                share, seq
            )
            for step in steps
        ]
        contexts = [pieces[0]] + [shifted(p, step) for p, step in zip(pieces[1:], steps[1:])]
        across, straight, _ = lax.optimization_barrier((across, straight, pieces[0]))
        half = seq // 2
        corner = [
            jnp.concatenate(
                [shifted(piece[:half], (1, 0, 0)), shifted(across[half:], (0, 0, r))]
            )
            for r, piece in enumerate(straight, 1)
        ]
        near = {(0, 0): first, (1, 0): across}
        for r in range(1, replicas):
            near[0, r], near[1, r] = straight[r - 1], corner[r - 1]
        outputs = [
            near[x, r] if c == 0 else shifted(near[x, r], (0, 1, 0)) for x, c, r in steps
        ]
        kept.append((outputs, contexts))
    terms = weight_terms(
        [c for pair in kept for c in pair[1]], [o for pair in kept for o in pair[0]]
    )
    total = lax.psum_scatter(terms, "z", scatter_dimension=0, tiled=True)
    results = []
    for image in range(image_count):
        grad = jnp.zeros((depth, *extents, slab, seq), jnp.bfloat16)
        for step, output in zip(steps, kept[image][0]):
            piece = dot(weight, output, ((1,), (1,))).astype(jnp.bfloat16)
            if any(step):
                piece = shifted(piece, tuple(-s for s in step))
            grad = lax.dynamic_update_slice(
                grad, piece.reshape(depth, 1, 1, 1, slab, seq), start_at(step)
            )
        results.append(
            backward(queries[image], keys[image], values[image], grad.reshape(rows, seq))
        )
    grads = [
        parts[0][None] if image_count == 1 else jnp.stack(parts) for parts in zip(*results)
    ]
    return (*grads, total.astype(jnp.float32))


def solution(mesh):
    groups, replicas = mesh.shape["group"], mesh.shape["rep"]
    split = Mesh(
        mesh.devices.reshape(groups // (2 * CORES), 2, CORES, replicas), ("z", *PLANE)
    )
    images = P(("z", *PLANE), None, None)
    shards = P(("z", "x", "core"), None)
    return jax.shard_map(
        per_device,
        mesh=split,
        in_specs=(images,) * 4 + (shards,) * 2,
        out_specs=(images,) * 3 + (P(("z", *PLANE), None),),
        check_vma=False,
    )
```
